32 devices in a mesh: dp: 4 (over y, x), mx: 4 (over z), my: 2 (over core).
Axes of the slice: x: 2, y: 2, z: 4, core: 2. Of those that a mesh axis runs over, the one named last changes fastest.
Arguments:
- tokens: bfloat16 [8192, 2048], P(('dp', 'my'), 'mx'), may hold values from -6 to 6
- output_grad: bfloat16 [8192, 2048], P(('dp', 'my'), 'mx'), may hold values from -6 to 6
- picture_starts: int32 [8, 2], P('dp'), may hold values from 0 to 768, as said below
- norm1_gain: float32 [2048], P('mx'), may hold values from 0.5 to 1.5
- query_weight: bfloat16 [2048, 2048], P('mx', 'my'), may hold values from -0.5 to 0.5
- key_weight: bfloat16 [2048, 512], P('mx', 'my'), may hold values from -0.5 to 0.5
- value_weight: bfloat16 [2048, 512], P('mx', 'my'), may hold values from -0.125 to 0.125
- out_weight: bfloat16 [2048, 2048], P('my', 'mx'), may hold values from -2 to 2
- norm2_gain: float32 [2048], P('mx'), may hold values from 0.5 to 1.5
- gate_weight: bfloat16 [2048, 8192], P('mx', 'my'), may hold values from -0.125 to 0.125
- up_weight: bfloat16 [2048, 8192], P('mx', 'my'), may hold values from -0.125 to 0.125
- down_weight: bfloat16 [8192, 2048], P('my', 'mx'), may hold values from -0.5 to 0.5
Outputs:
- output: bfloat16 [8192, 2048], P(('dp', 'my'), 'mx')
- input_grad: bfloat16 [8192, 2048], P(('dp', 'my'), 'mx')
- grad_norm1: float32 [2048], P('mx')
- grad_query: float32 [2048, 2048], P('mx', 'my')
- grad_key: float32 [2048, 512], P('mx', 'my')
- grad_value: float32 [2048, 512], P('mx', 'my')
- grad_out: float32 [2048, 2048], P('my', 'mx')
- grad_norm2: float32 [2048], P('mx')
- grad_gate: float32 [2048, 8192], P('mx', 'my')
- grad_up: float32 [2048, 8192], P('mx', 'my')
- grad_down: float32 [8192, 2048], P('my', 'mx')
The draws below stay inside these ranges and needn't reach their ends.
Inputs may be any that keep to these rules, and one draw needn't show every extreme that they name: `picture_starts`: piece p of a sequence starts at a position from p * 512 to (p + 1) * 512 - 256, so the pieces of a sequence never intersect and lie inside it; some sequence has its first piece at position 0 and some sequence has its last piece ending at the sequence's end.
All inputs are finite; a program needn't handle non-finite values.
Results may differ from the reference program's by a relative error of at most 0.02.
Values may be sent and summed in bfloat16 or wider, within the bound.
No kernel may reach another device: no remote copies, remote signals or barrier semaphores. Data moves between devices by JAX's collectives and lax.ppermute only.
A program may use at most 384 MiB of HBM per device.

```python
import jax
import jax.numpy as jnp
from jax import lax

D = 2048
QH = 32
KVH = 8
HEAD = 64
FF = 8192
LEN = 1024
PIECE = 256
PIECES = 2
SEQ_DEV = 2
SEQS = 8
TOKENS = 8192
N_DP = 4


def draw_picture_starts(key, part):
    span_length = LEN // PIECES
    offsets = jax.random.randint(jax.random.fold_in(key, 1), (SEQS, PIECES), 0, span_length - PIECE + 1)
    first_row = jax.random.randint(jax.random.fold_in(key, 2), (), 0, SEQS)
    last_row = jax.random.randint(jax.random.fold_in(key, 3), (), 0, SEQS)
    row_ids = jnp.arange(SEQS, dtype=jnp.int32)
    piece_ids = jnp.arange(PIECES, dtype=jnp.int32)
    low_end = (row_ids[:, None] == first_row) & (piece_ids[None, :] == 0)
    high_end = (row_ids[:, None] == last_row) & (piece_ids[None, :] == PIECES - 1)
    offsets = jnp.where(low_end, 0, offsets)
    offsets = jnp.where(high_end, span_length - PIECE, offsets)
    firsts = piece_ids * span_length
    return (offsets + firsts[None, :]).astype(jnp.int32)


def shard_levels(key, extent, pieces, low, high):
    factor_of = 1.0
    for dim, blocks in pieces:
        heights = jax.random.uniform(jax.random.fold_in(jax.random.fold_in(key, 6), dim), (blocks,), jnp.float32, low / len(pieces), high / len(pieces))
        factor_of = factor_of * jnp.repeat(jnp.exp(heights), extent[dim] // blocks).reshape((-1,) + (1,) * (len(extent) - 1 - dim))
    return factor_of


def bell_draw(rng, extent, width, limit, pieces=(), held_as=jnp.bfloat16):
    drawn = width * jax.random.normal(rng, extent, jnp.float32)
    if pieces:
        drawn = drawn * shard_levels(rng, extent, pieces, -0.22, 0.18)
    return jnp.clip(drawn, -limit, limit).astype(held_as)


def setup_inputs(seed: int = 0) -> dict:
    key_of = jax.random.split(jax.random.key(seed), 13)
    return {
        "tokens": bell_draw(key_of[0], (TOKENS, D), 1.0, 6.0, ((0, 8), (1, 4))),
        "output_grad": bell_draw(key_of[1], (TOKENS, D), 1.0, 6.0, ((0, 8), (1, 4))),
        "picture_starts": draw_picture_starts(jax.random.fold_in(key_of[12], 71), 0),
        "norm1_gain": jnp.clip(1.0 + 0.1 * jax.random.normal(key_of[3], (D,), jnp.float32), 0.5, 1.5),
        "query_weight": bell_draw(key_of[4], (D, QH * HEAD), (D // 16) ** -0.5, 0.5, ((0, 4), (1, 2))),
        "key_weight": bell_draw(key_of[5], (D, KVH * HEAD), (D // 16) ** -0.5, 0.5, ((0, 4), (1, 2))),
        "value_weight": bell_draw(key_of[6], (D, KVH * HEAD), D ** -0.5, 0.125, ((0, 4), (1, 2))),
        "out_weight": bell_draw(key_of[7], (QH * HEAD, D), 8 ** -0.5, 2.0, ((0, 2), (1, 4))),
        "norm2_gain": jnp.clip(1.0 + 0.1 * jax.random.normal(key_of[8], (D,), jnp.float32), 0.5, 1.5),
        "gate_weight": bell_draw(key_of[9], (D, FF), D ** -0.5, 0.125, ((0, 4), (1, 2))),
        "up_weight": bell_draw(key_of[10], (D, FF), D ** -0.5, 0.125, ((0, 4), (1, 2))),
        "down_weight": bell_draw(key_of[11], (FF, D), (FF // 64) ** -0.5, 0.5, ((0, 2), (1, 4))),
    }


epsilon = 1e-05
rope_base = 10000000.0
branch_scale = 0.22
score_scale = 0.015625
masked_score = -1e+30
highest = lax.Precision.HIGHEST

@jax.custom_vjp
def low(v):
    return lax.optimization_barrier(v.astype(jnp.bfloat16)).astype(jnp.float32)

@jax.custom_vjp
def low_back(v):
    return v

def low_keep(v):
    return (low(v), None)

def low_pass(kept, grad):
    return (grad,)

def back_keep(v):
    return (v, None)

def back_low(kept, grad):
    return (low(grad),)
low.defvjp(low_keep, low_pass)
low_back.defvjp(back_keep, back_low)

def rope_tables(positions, head_width):
    half_width = head_width // 2
    steps_idx = jnp.arange(half_width, dtype=jnp.float32)
    freqs = jnp.exp(-jnp.log(jnp.float32(rope_base)) * 2.0 * steps_idx / head_width)
    angles = positions.astype(jnp.float32)[:, None] * freqs[None, :]
    cosine = jnp.cos(angles)
    sine = jnp.sin(angles)
    return (jnp.concatenate([cosine, cosine], 1), jnp.concatenate([sine, sine], 1))

def rotate_half(values):
    half_width = values.shape[-1] // 2
    return jnp.concatenate([-values[..., half_width:], values[..., :half_width]], -1)

def apply_rope(values, cosine, sine):
    return values * cosine[:, None, :] + rotate_half(values) * sine[:, None, :]

def row_info(row_ids, starts, seq_length, piece_length):
    sequence_ids = row_ids // seq_length
    position = row_ids % seq_length
    choose_row = (sequence_ids[:, None] == jnp.arange(starts.shape[0], dtype=jnp.int32)[None, :]).astype(jnp.int32)
    piece_begin = lax.optimization_barrier(jnp.sum(choose_row[:, :, None] * starts[None, :, :], axis=1))
    inside = (position[:, None] >= piece_begin) & (position[:, None] < piece_begin + piece_length)
    number = jnp.arange(1, starts.shape[1] + 1, dtype=jnp.int32)
    piece_id = lax.optimization_barrier(jnp.sum(inside.astype(jnp.int32) * number[None, :], axis=1)) - 1
    return (sequence_ids, position, piece_id)

def allowed(query_facts, key_facts):
    query_seq, query_pos, query_piece = query_facts
    key_seq, key_pos, key_piece = key_facts
    same_sequence = query_seq[:, None] == key_seq[None, :]
    before = key_pos[None, :] <= query_pos[:, None]
    piece_both = (query_piece[:, None] >= 0) & (query_piece[:, None] == key_piece[None, :])
    return same_sequence & (before | piece_both)

def matmul_hi(left, right):
    return jnp.dot(left, right, precision=highest, preferred_element_type=jnp.float32)

def attend(head_parts):
    query_rows, key_rows, value_rows, starts = head_parts
    row_ids = jnp.arange(LEN, dtype=jnp.int32)
    row_facts = row_info(row_ids, starts[None, :], LEN, PIECE)
    allowed_pairs = allowed(row_facts, row_facts)
    grouped = query_rows.reshape(LEN, KVH, QH // KVH, HEAD)
    scores = jnp.einsum('qhgd,khd->hgqk', grouped, key_rows, precision=highest) * score_scale
    scores = low_back(scores)
    scores = jnp.where(allowed_pairs[None, None, :, :], scores, masked_score)
    row_max = lax.optimization_barrier(jnp.max(scores, axis=-1, keepdims=True))
    shifted = jnp.exp(scores - row_max)
    probs = shifted / lax.optimization_barrier(jnp.sum(shifted, axis=-1, keepdims=True))
    mixed = jnp.einsum('hgqk,khd->qhgd', low(probs), value_rows, precision=highest)
    return mixed.reshape(LEN, QH * HEAD)

def forward(stream, gain_one, query_w, key_w, value_w, out_w, gain_two, gate_w, up_w, down_w, starts):
    row_count = stream.shape[0]
    seq_count = row_count // LEN
    inverse_one = lax.rsqrt(lax.optimization_barrier(jnp.mean(stream * stream, axis=1, keepdims=True)) + epsilon)
    normed_one = low(stream * inverse_one * gain_one[None, :])
    query_pre = low_back(matmul_hi(normed_one, query_w))
    key_pre = low_back(matmul_hi(normed_one, key_w))
    value_all = low(low_back(matmul_hi(normed_one, value_w)))
    positions = jnp.arange(row_count, dtype=jnp.int32) % LEN
    cosine, sine = rope_tables(positions, HEAD)
    query_all = low(apply_rope(query_pre.reshape(row_count, QH, HEAD), cosine, sine))
    key_all = low(apply_rope(key_pre.reshape(row_count, KVH, HEAD), cosine, sine))
    value_all = value_all.reshape(row_count, KVH, HEAD)
    attend_saved = jax.checkpoint(attend)
    mixed = lax.map(attend_saved, (query_all.reshape(seq_count, LEN, QH, HEAD), key_all.reshape(seq_count, LEN, KVH, HEAD), value_all.reshape(seq_count, LEN, KVH, HEAD), starts))
    attn_out = low(low_back(mixed.reshape(row_count, QH * HEAD)))
    hidden_one = stream + branch_scale * low_back(matmul_hi(attn_out, out_w))
    inverse_two = lax.rsqrt(lax.optimization_barrier(jnp.mean(hidden_one * hidden_one, axis=1, keepdims=True)) + epsilon)
    normed_two = low(hidden_one * inverse_two * gain_two[None, :])
    gate_val = low_back(matmul_hi(normed_two, gate_w))
    up_val = low_back(matmul_hi(normed_two, up_w))
    hidden_units = low(jax.nn.silu(gate_val) * up_val)
    return hidden_one + branch_scale * low_back(matmul_hi(hidden_units, down_w))

def reference(tokens, output_grad, picture_starts, norm1_gain, query_weight, key_weight, value_weight, out_weight, norm2_gain, gate_weight, up_weight, down_weight):
    weights = tuple((item.astype(jnp.float32) for item in (norm1_gain, query_weight, key_weight, value_weight, out_weight, norm2_gain, gate_weight, up_weight, down_weight)))
    group_rows = SEQ_DEV * LEN
    streams = tokens.astype(jnp.float32).reshape(N_DP, group_rows, D)
    cotangents = output_grad.astype(jnp.float32).reshape(N_DP, group_rows, D)
    starts_all = picture_starts.reshape(N_DP, SEQ_DEV, PIECES)

    def one_group(totals, group_parts):
        stream, cotangent, starts = group_parts

        def layer(inputs, *params):
            return forward(inputs, *params, starts)
        result, pullback = jax.vjp(layer, stream, *weights)
        grads = pullback(cotangent)
        totals = tuple((total + grad for total, grad in zip(totals, grads[1:])))
        return (totals, (result.astype(jnp.bfloat16), grads[0].astype(jnp.bfloat16)))
    zeros_all = tuple((jnp.zeros_like(item) for item in weights))
    totals, (outputs, input_grads) = lax.scan(one_group, zeros_all, (streams, cotangents, starts_all))
    return (outputs.reshape(TOKENS, D), input_grads.reshape(TOKENS, D), totals[0], totals[1], totals[2], totals[3], totals[4], totals[5], totals[6], totals[7], totals[8])
```

```python
import jax
import jax.numpy as jnp
from jax import lax
from jax.sharding import PartitionSpec as P

D = 2048
HEAD = 64
LEN = 1024
PIECE = 256


epsilon = 1e-05
rope_base = 10000000.0
branch_scale = 0.22
score_scale = 0.015625
masked_score = -1e30


def rope_tables(positions, head_width):
    half_width = head_width // 2
    steps_idx = jnp.arange(half_width, dtype=jnp.float32)
    freqs = jnp.exp(-jnp.log(jnp.float32(rope_base)) * 2.0 * steps_idx / head_width)
    angles = positions.astype(jnp.float32)[:, None] * freqs[None, :]
    cosine = jnp.cos(angles)
    sine = jnp.sin(angles)
    return (jnp.concatenate([cosine, cosine], 1), jnp.concatenate([sine, sine], 1))


def rotate_half(values):
    half_width = values.shape[-1] // 2
    return jnp.concatenate([-values[..., half_width:], values[..., :half_width]], -1)


def apply_rope(values, cosine, sine):
    return values * cosine + rotate_half(values) * sine


def rope_back(values, cosine, sine):
    return values * cosine - rotate_half(values) * sine


def product(left, weight, flipped):
    if flipped:
        return lax.dot_general(
            left, weight, (((1,), (1,)), ((), ())), preferred_element_type=jnp.float32
        )
    return jnp.dot(left, weight, preferred_element_type=jnp.float32)


def outer_sum(left, right):
    return lax.dot_general(
        left, right, (((0,), (0,)), ((), ())), preferred_element_type=jnp.float32
    )


def head_scores(query, key_head, allowed_pairs):
    scores = (
        jnp.einsum("qgd,kd->qgk", query, key_head, preferred_element_type=jnp.float32) * score_scale
    )
    return jnp.where(allowed_pairs[:, None, :], scores, masked_score)


def head_forward(query, key_head, value_head, allowed_pairs):
    scores = head_scores(query, key_head, allowed_pairs)
    row_max = jnp.max(scores, axis=-1, keepdims=True)
    shifted = jnp.exp(scores - row_max)
    row_total = jnp.sum(shifted, axis=-1, keepdims=True)
    probs = shifted / row_total
    mixed = jnp.einsum(
        "qgk,kd->qgd", probs.astype(jnp.bfloat16), value_head, preferred_element_type=jnp.float32
    )
    return (mixed, (row_max + jnp.log(row_total))[..., 0])


def head_backward(query, key_head, value_head, grad_out, log_total, allowed_pairs):
    scores = head_scores(query, key_head, allowed_pairs)
    probs = jnp.exp(scores - log_total[..., None])
    grad_probs = jnp.einsum("qgd,kd->qgk", grad_out, value_head, preferred_element_type=jnp.float32)
    row_dot = jnp.sum(probs * grad_probs, axis=-1, keepdims=True)
    grad_scores = (probs * (grad_probs - row_dot)).astype(jnp.bfloat16)
    grad_query = (
        jnp.einsum("qgk,kd->qgd", grad_scores, key_head, preferred_element_type=jnp.float32)
        * score_scale
    )
    grad_key = (
        jnp.einsum("qgk,qgd->kd", grad_scores, query, preferred_element_type=jnp.float32)
        * score_scale
    )
    grad_value = jnp.einsum(
        "qgk,qgd->kd", probs.astype(jnp.bfloat16), grad_out, preferred_element_type=jnp.float32
    )
    return (grad_query, grad_key, grad_value)


PLANE = ("dp", "my")


def plane_gather(values):
    return lax.all_gather(values, PLANE, axis=0, tiled=True)


def plane_scatter(values):
    return lax.psum_scatter(
        values.astype(jnp.bfloat16), PLANE, scatter_dimension=0, tiled=True
    ).astype(jnp.float32)


def to_rows(values):
    return lax.all_to_all(values, "mx", split_axis=0, concat_axis=1, tiled=True)


def to_tiles(values):
    return lax.all_to_all(values, "mx", split_axis=1, concat_axis=0, tiled=True)


def line_gather(values, axis):
    return lax.all_gather(values, "mx", axis=axis, tiled=True)


def line_scatter(values, axis):
    return lax.psum_scatter(
        values.astype(jnp.bfloat16), "mx", scatter_dimension=axis, tiled=True
    )


def norm_forward(stream, gain):
    mean = jnp.mean(stream * stream, axis=1, keepdims=True)
    inverse = lax.rsqrt(mean + epsilon)
    return (inverse, (stream * inverse * gain[None, :]).astype(jnp.bfloat16))


def norm_backward(stream, inverse, gain, grad_normed):
    scaled = gain[None, :] * grad_normed
    row_mean = jnp.mean(stream * scaled, axis=1, keepdims=True)
    grad_stream = inverse * scaled - stream * inverse * inverse * inverse * row_mean
    grad_gain = jnp.sum(grad_normed * stream * inverse, axis=0)
    return (grad_stream, grad_gain)


def piece_of(position, begins):
    inside = (position >= begins) & (position < begins + PIECE)
    number = jnp.arange(1, begins.shape[-1] + 1, dtype=jnp.int32)
    return jnp.sum(jnp.where(inside, number, 0), axis=-1)


def shards(
    tokens,
    output_grad,
    picture_starts,
    norm1_gain,
    query_weight,
    key_weight,
    value_weight,
    out_weight,
    norm2_gain,
    gate_weight,
    up_weight,
    down_weight,
):
    mx_count = lax.axis_size("mx")
    dp_count = lax.axis_size("dp")
    dp_index = lax.axis_index("dp")
    mx_index = lax.axis_index("mx")
    chunk = LEN // mx_count
    seqs = dp_count * lax.axis_size("my")
    rows = seqs * chunk
    query_cols = query_weight.shape[1] // dp_count
    query_heads = query_cols // HEAD
    key_heads = key_weight.shape[1] // HEAD
    share = max(1, dp_count // key_heads)
    key_cols = key_weight.shape[1] * share // dp_count
    own_keys = key_cols // HEAD
    kv_group = query_heads // own_keys
    hidden = gate_weight.shape[1] // dp_count

    def cols(weight, width, index):
        return lax.dynamic_slice_in_dim(weight, index * width, width, axis=1)

    def rows_of(weight, width):
        return lax.dynamic_slice_in_dim(weight, dp_index * width, width, axis=0)

    key_index = dp_index // share
    attn_in = line_gather(
        jnp.concatenate(
            [
                cols(query_weight, query_cols, dp_index),
                cols(key_weight, key_cols, key_index),
                cols(value_weight, key_cols, key_index),
            ],
            axis=1,
        ),
        0,
    )
    attn_back = line_gather(rows_of(out_weight, query_cols), 1)
    ffn_in = line_gather(
        jnp.concatenate(
            [cols(gate_weight, hidden, dp_index), cols(up_weight, hidden, dp_index)], axis=1
        ),
        0,
    )
    ffn_back = line_gather(rows_of(down_weight, hidden), 1)
    gains = line_gather(jnp.stack([norm1_gain, norm2_gain]), 1)
    gain_one, gain_two = gains[0], gains[1]
    starts = lax.all_gather(picture_starts, "dp", axis=0, tiled=True)

    stream = to_rows(tokens).astype(jnp.float32)
    grad_two = to_rows(output_grad).astype(jnp.float32)
    inverse_one, normed_one = norm_forward(stream, gain_one)
    normed_one_all = plane_gather(normed_one)
    projected = product(normed_one_all, attn_in, False)

    query_pos = mx_index * chunk + jnp.arange(chunk, dtype=jnp.int32)
    key_pos = jnp.arange(LEN, dtype=jnp.int32)
    cosine, sine = rope_tables(query_pos, HEAD)
    cosine = cosine[None, :, None, :]
    sine = sine[None, :, None, :]
    query_piece = piece_of(query_pos[None, :, None], starts[:, None, :])
    key_piece = piece_of(key_pos[None, :, None], starts[:, None, :])
    before = key_pos[None, None, :] <= query_pos[None, :, None]
    same = (query_piece[:, :, None] > 0) & (query_piece[:, :, None] == key_piece[:, None, :])
    allowed_pairs = before | same

    query_rot = apply_rope(
        projected[:, :query_cols].reshape(seqs, chunk, query_heads, HEAD), cosine, sine
    ).astype(jnp.bfloat16)
    key_rot = apply_rope(
        projected[:, query_cols : query_cols + key_cols].reshape(seqs, chunk, own_keys, HEAD),
        cosine,
        sine,
    ).astype(jnp.bfloat16)
    value_own = projected[:, query_cols + key_cols :].astype(jnp.bfloat16)
    key_local = jnp.concatenate(
        [key_rot.reshape(seqs, chunk, key_cols), value_own.reshape(seqs, chunk, key_cols)], axis=2
    )
    key_all = line_gather(key_local, 1)

    query_split = query_rot.reshape(seqs, chunk, own_keys, kv_group, HEAD)
    query_split = query_split.transpose(0, 2, 1, 3, 4).reshape(-1, chunk, kv_group, HEAD)

    def split_keys(values):
        values = values.reshape(seqs, LEN, own_keys, HEAD)
        return values.transpose(0, 2, 1, 3).reshape(-1, LEN, HEAD)

    key_split = split_keys(key_all[:, :, :key_cols])
    value_split = split_keys(key_all[:, :, key_cols:])
    pairs = jnp.repeat(allowed_pairs, own_keys, axis=0)
    mixed, log_totals = lax.map(
        lambda p: head_forward(p[0], p[1], p[2], p[3]),
        (query_split, key_split, value_split, pairs),
    )

    def join_heads(values):
        values = values.reshape(seqs, own_keys, chunk, kv_group, HEAD).transpose(0, 2, 1, 3, 4)
        return values.reshape(rows, query_cols)

    def split_heads(values):
        values = values.reshape(seqs, chunk, own_keys, kv_group, HEAD).transpose(0, 2, 1, 3, 4)
        return values.reshape(-1, chunk, kv_group, HEAD)

    attn_out = join_heads(mixed).astype(jnp.bfloat16)
    hidden_one = stream + branch_scale * plane_scatter(product(attn_out, attn_back, False))
    inverse_two, normed_two = norm_forward(hidden_one, gain_two)
    normed_two_all = plane_gather(normed_two)
    gate_up = product(normed_two_all, ffn_in, False)
    gate_val = gate_up[:, :hidden]
    up_val = gate_up[:, hidden:]
    sigma = jax.nn.sigmoid(gate_val)
    silu_gate = gate_val * sigma
    hidden_units = (silu_gate * up_val).astype(jnp.bfloat16)
    hidden_two = hidden_one + branch_scale * plane_scatter(product(hidden_units, ffn_back, False))
    output = to_tiles(hidden_two.astype(jnp.bfloat16))

    branch_two = (branch_scale * grad_two).astype(jnp.bfloat16)
    branch_two_all = plane_gather(branch_two)
    grad_down = outer_sum(hidden_units, branch_two_all)
    grad_hidden = product(branch_two_all, ffn_back, True)
    grad_gate_val = (grad_hidden * up_val * sigma * (1.0 + gate_val * (1.0 - sigma))).astype(
        jnp.bfloat16
    )
    grad_up_val = (grad_hidden * silu_gate).astype(jnp.bfloat16)
    grad_gate_up = jnp.concatenate([grad_gate_val, grad_up_val], axis=1)
    grad_ffn_in = outer_sum(normed_two_all, grad_gate_up)
    grad_normed_two = plane_scatter(product(grad_gate_up, ffn_in, True))
    grad_stream_two, grad_norm2 = norm_backward(hidden_one, inverse_two, gain_two, grad_normed_two)
    grad_one = grad_two + grad_stream_two
    branch_one_all = plane_gather((branch_scale * grad_one).astype(jnp.bfloat16))
    grad_out = outer_sum(attn_out, branch_one_all)
    grad_attn = split_heads(product(branch_one_all, attn_back, True).astype(jnp.bfloat16))
    grad_q, grad_k, grad_v = lax.map(
        lambda p: head_backward(p[0], p[1], p[2], p[3], p[4], p[5]),
        (query_split, key_split, value_split, grad_attn, log_totals, pairs),
    )

    def join_keys(values):
        values = values.reshape(seqs, own_keys, LEN, HEAD).transpose(0, 2, 1, 3)
        return values.reshape(seqs, LEN, key_cols)

    key_terms = jnp.concatenate([join_keys(grad_k), join_keys(grad_v)], axis=2)
    key_owned = line_scatter(key_terms, 1).astype(jnp.float32)
    grad_q_pre = rope_back(
        join_heads(grad_q).reshape(seqs, chunk, query_heads, HEAD), cosine, sine
    )
    grad_k_pre = rope_back(
        key_owned[:, :, :key_cols].reshape(seqs, chunk, own_keys, HEAD), cosine, sine
    )
    grad_projected = jnp.concatenate(
        [
            grad_q_pre.reshape(rows, query_cols),
            grad_k_pre.reshape(rows, key_cols),
            key_owned[:, :, key_cols:].reshape(rows, key_cols),
        ],
        axis=1,
    ).astype(jnp.bfloat16)
    grad_attn_in = outer_sum(normed_one_all, grad_projected)
    grad_normed_one = plane_scatter(product(grad_projected, attn_in, True))
    grad_stream_one, grad_norm1 = norm_backward(stream, inverse_one, gain_one, grad_normed_one)
    input_grad = to_tiles((grad_one + grad_stream_one).astype(jnp.bfloat16))

    def spread_cols(own):
        return lax.all_gather(own, "dp", axis=1, tiled=True).astype(jnp.float32)

    def spread_rows(own):
        return lax.all_gather(own, "dp", axis=0, tiled=True).astype(jnp.float32)

    def spread_keys(own):
        every = lax.all_gather(own, "dp", axis=0).astype(jnp.float32)
        every = every.reshape(dp_count // share, share, -1, key_cols).sum(axis=1)
        return every.transpose(1, 0, 2).reshape(every.shape[1], -1)

    grad_down = spread_rows(line_scatter(grad_down, 1))
    own_ffn = line_scatter(grad_ffn_in, 0)
    grad_gate = spread_cols(own_ffn[:, :hidden])
    grad_up = spread_cols(own_ffn[:, hidden:])
    grad_out = spread_rows(line_scatter(grad_out, 1))
    own_attn = line_scatter(grad_attn_in, 0)
    grad_query = spread_cols(own_attn[:, :query_cols])
    grad_key = spread_keys(own_attn[:, query_cols : query_cols + key_cols])
    grad_value = spread_keys(own_attn[:, query_cols + key_cols :])
    norms = lax.psum(jnp.stack([grad_norm1, grad_norm2]), ("dp", "mx", "my"))
    norms = lax.dynamic_slice_in_dim(norms, mx_index * norm1_gain.shape[0], norm1_gain.shape[0], 1)
    return (
        output,
        input_grad,
        norms[0],
        grad_query,
        grad_key,
        grad_value,
        grad_out,
        norms[1],
        grad_gate,
        grad_up,
        grad_down,
    )


def solution(mesh):
    placed = (
        P(("dp", "my"), "mx"),
        P(("dp", "my"), "mx"),
        P("dp", None),
        P("mx"),
        P("mx", "my"),
        P("mx", "my"),
        P("mx", "my"),
        P("my", "mx"),
        P("mx"),
        P("mx", "my"),
        P("mx", "my"),
        P("my", "mx"),
    )
    return jax.shard_map(
        shards,
        mesh=mesh,
        in_specs=placed,
        out_specs=(
            P(("dp", "my"), "mx"),
            P(("dp", "my"), "mx"),
            P("mx"),
            P("mx", "my"),
            P("mx", "my"),
            P("mx", "my"),
            P("my", "mx"),
            P("mx"),
            P("mx", "my"),
            P("mx", "my"),
            P("my", "mx"),
        ),
        check_vma=False,
    )
```

```python
import jax
import jax.numpy as jnp
from jax import lax
from jax.sharding import PartitionSpec as P

D = 2048
HEAD = 64
LEN = 1024
PIECE = 256


epsilon = 1e-05
rope_base = 10000000.0
branch_scale = 0.22
score_scale = 0.015625
masked_score = -1e30


def rope_tables(positions, head_width):
    half_width = head_width // 2
    steps_idx = jnp.arange(half_width, dtype=jnp.float32)
    freqs = jnp.exp(-jnp.log(jnp.float32(rope_base)) * 2.0 * steps_idx / head_width)
    angles = positions.astype(jnp.float32)[:, None] * freqs[None, :]
    cosine = jnp.cos(angles)
    sine = jnp.sin(angles)
    return (jnp.concatenate([cosine, cosine], 1), jnp.concatenate([sine, sine], 1))


def rotate_half(values):
    half_width = values.shape[-1] // 2
    return jnp.concatenate([-values[..., half_width:], values[..., :half_width]], -1)


def apply_rope(values, cosine, sine):
    return values * cosine + rotate_half(values) * sine


def rope_back(values, cosine, sine):
    return values * cosine - rotate_half(values) * sine


def product(left, weight, flipped):
    if flipped:
        return lax.dot_general(
            left, weight, (((1,), (1,)), ((), ())), preferred_element_type=jnp.float32
        )
    return jnp.dot(left, weight, preferred_element_type=jnp.float32)


def outer_sum(left, right):
    return lax.dot_general(
        left, right, (((0,), (0,)), ((), ())), preferred_element_type=jnp.float32
    )


def head_scores(query, key_head, allowed_pairs):
    scores = (
        jnp.einsum("qgd,kd->qgk", query, key_head, preferred_element_type=jnp.float32) * score_scale
    )
    return jnp.where(allowed_pairs[:, None, :], scores, masked_score)


def head_forward(query, key_head, value_head, allowed_pairs):
    scores = head_scores(query, key_head, allowed_pairs)
    row_max = jnp.max(scores, axis=-1, keepdims=True)
    shifted = jnp.exp(scores - row_max)
    row_total = jnp.sum(shifted, axis=-1, keepdims=True)
    probs = shifted / row_total
    mixed = jnp.einsum(
        "qgk,kd->qgd", probs.astype(jnp.bfloat16), value_head, preferred_element_type=jnp.float32
    )
    return (mixed, (row_max + jnp.log(row_total))[..., 0])


def head_backward(query, key_head, value_head, grad_out, log_total, allowed_pairs):
    scores = head_scores(query, key_head, allowed_pairs)
    probs = jnp.exp(scores - log_total[..., None])
    grad_probs = jnp.einsum("qgd,kd->qgk", grad_out, value_head, preferred_element_type=jnp.float32)
    row_dot = jnp.sum(probs * grad_probs, axis=-1, keepdims=True)
    grad_scores = (probs * (grad_probs - row_dot)).astype(jnp.bfloat16)
    grad_query = (
        jnp.einsum("qgk,kd->qgd", grad_scores, key_head, preferred_element_type=jnp.float32)
        * score_scale
    )
    grad_key = (
        jnp.einsum("qgk,qgd->kd", grad_scores, query, preferred_element_type=jnp.float32)
        * score_scale
    )
    grad_value = jnp.einsum(
        "qgk,qgd->kd", probs.astype(jnp.bfloat16), grad_out, preferred_element_type=jnp.float32
    )
    return (grad_query, grad_key, grad_value)


PLANE = ("dp", "my")


def swap(values, bit):
    count = lax.axis_size("dp")
    return lax.ppermute(values, "dp", [(i, i ^ bit) for i in range(count)])


def swap_core(values):
    count = lax.axis_size("my")
    return lax.ppermute(values, "my", [(i, i ^ 1) for i in range(count)])


def small_plane():
    return lax.axis_size("dp") == 4 and lax.axis_size("my") == 2


def plane_gather(values):
    if not small_plane():
        return lax.all_gather(values, PLANE, axis=0, tiled=True)
    half = values.shape[0] // 2
    from_x = swap(values, 1)
    from_y = swap(values, 2)
    core_own = swap_core(values)
    corner_low = swap(from_y[:half], 1)
    corner_high = swap(from_x[half:], 2)
    core_x = swap_core(from_x)
    core_y = swap_core(from_y)
    corner = jnp.concatenate([corner_low, corner_high], axis=0)
    core_corner = swap_core(corner)
    return jnp.concatenate(
        [values, from_x, from_y, corner, core_own, core_x, core_y, core_corner], axis=0
    )


def plane_scatter(left, weight, flipped):
    if not small_plane():
        return lax.psum_scatter(
            product(left, weight, flipped).astype(jnp.bfloat16),
            PLANE,
            scatter_dimension=0,
            tiled=True,
        ).astype(jnp.float32)
    rows = left.shape[0] // 8
    half = rows // 2
    low = jnp.bfloat16
    wide = jnp.float32
    other = product(left[4 * rows :], weight, flipped).astype(low)
    got = [swap_core(other[k * rows : (k + 1) * rows]) for k in range(4)]
    own = product(left[: 4 * rows], weight, flipped).astype(low)
    part = [
        own[k * rows : (k + 1) * rows].astype(wide) + got[k].astype(wide) for k in range(4)
    ]
    via_x = swap(jnp.concatenate([part[3][:half], part[1][:half]], 0).astype(low), 1).astype(wide)
    via_y = swap(jnp.concatenate([part[3][half:], part[2][half:]], 0).astype(low), 2).astype(wide)
    next_y = swap((part[2][:half] + via_x[:half]).astype(low), 2)
    next_x = swap((part[1][half:] + via_y[:half]).astype(low), 1)
    first = part[0][:half] + via_x[half:] + next_y.astype(wide)
    second = part[0][half:] + via_y[half:] + next_x.astype(wide)
    return jnp.concatenate([first, second], axis=0)


def plane_order(values):
    if not small_plane():
        return values.reshape((-1,) + values.shape[2:])
    dp_index = lax.axis_index("dp")
    my_index = lax.axis_index("my")
    blocks = [values[dp_index ^ k, my_index ^ l] for l in range(2) for k in range(4)]
    return jnp.stack(blocks)


def line_exchange(blocks):
    count = lax.axis_size("mx")
    index = lax.axis_index("mx")

    def at(offset):
        return lax.dynamic_index_in_dim(blocks, (index + offset) % count, 0, keepdims=False)

    result = jnp.zeros_like(blocks)
    result = lax.dynamic_update_index_in_dim(result, at(0), index, 0)
    for shift in range(1, count):
        moved = lax.ppermute(at(shift), "mx", [(i, (i + shift) % count) for i in range(count)])
        result = lax.dynamic_update_index_in_dim(result, moved, (index - shift) % count, 0)
    return result


def to_rows(values):
    count = lax.axis_size("mx")
    blocks = line_exchange(values.reshape(count, -1, values.shape[1]))
    return blocks.transpose(1, 0, 2).reshape(blocks.shape[1], -1)


def to_tiles(values):
    count = lax.axis_size("mx")
    blocks = values.reshape(values.shape[0], count, -1).transpose(1, 0, 2)
    return line_exchange(blocks).reshape(-1, blocks.shape[2])


def line_gather(values, axis):
    return lax.all_gather(values, "mx", axis=axis, tiled=True)


def line_scatter(values, axis):
    return lax.psum_scatter(
        values.astype(jnp.bfloat16), "mx", scatter_dimension=axis, tiled=True
    )


def norm_forward(stream, gain):
    mean = jnp.mean(stream * stream, axis=1, keepdims=True)
    inverse = lax.rsqrt(mean + epsilon)
    return (inverse, (stream * inverse * gain[None, :]).astype(jnp.bfloat16))


def norm_backward(stream, inverse, gain, grad_normed):
    scaled = gain[None, :] * grad_normed
    row_mean = jnp.mean(stream * scaled, axis=1, keepdims=True)
    grad_stream = inverse * scaled - stream * inverse * inverse * inverse * row_mean
    grad_gain = jnp.sum(grad_normed * stream * inverse, axis=0)
    return (grad_stream, grad_gain)


def piece_of(position, begins):
    inside = (position >= begins) & (position < begins + PIECE)
    number = jnp.arange(1, begins.shape[-1] + 1, dtype=jnp.int32)
    return jnp.sum(jnp.where(inside, number, 0), axis=-1)


def shards(
    tokens,
    output_grad,
    picture_starts,
    norm1_gain,
    query_weight,
    key_weight,
    value_weight,
    out_weight,
    norm2_gain,
    gate_weight,
    up_weight,
    down_weight,
):
    mx_count = lax.axis_size("mx")
    dp_count = lax.axis_size("dp")
    dp_index = lax.axis_index("dp")
    mx_index = lax.axis_index("mx")
    chunk = LEN // mx_count
    seqs = dp_count * lax.axis_size("my")
    rows = seqs * chunk
    query_cols = query_weight.shape[1] // dp_count
    query_heads = query_cols // HEAD
    key_heads = key_weight.shape[1] // HEAD
    share = max(1, dp_count // key_heads)
    key_cols = key_weight.shape[1] * share // dp_count
    own_keys = key_cols // HEAD
    kv_group = query_heads // own_keys
    hidden = gate_weight.shape[1] // dp_count

    def cols(weight, width, index):
        return lax.dynamic_slice_in_dim(weight, index * width, width, axis=1)

    def rows_of(weight, width):
        return lax.dynamic_slice_in_dim(weight, dp_index * width, width, axis=0)

    key_index = dp_index // share
    attn_in = line_gather(
        jnp.concatenate(
            [
                cols(query_weight, query_cols, dp_index),
                cols(key_weight, key_cols, key_index),
                cols(value_weight, key_cols, key_index),
            ],
            axis=1,
        ),
        0,
    )
    attn_back = line_gather(rows_of(out_weight, query_cols), 1)
    ffn_in = line_gather(
        jnp.concatenate(
            [cols(gate_weight, hidden, dp_index), cols(up_weight, hidden, dp_index)], axis=1
        ),
        0,
    )
    ffn_back = line_gather(rows_of(down_weight, hidden), 1)
    gains = line_gather(jnp.stack([norm1_gain, norm2_gain]), 1)
    gain_one, gain_two = gains[0], gains[1]
    starts = plane_order(lax.all_gather(picture_starts, "dp", axis=0))

    stream = to_rows(tokens).astype(jnp.float32)
    grad_two = to_rows(output_grad).astype(jnp.float32)
    inverse_one, normed_one = norm_forward(stream, gain_one)
    normed_one_all = plane_gather(normed_one)
    projected = product(normed_one_all, attn_in, False)

    query_pos = mx_index * chunk + jnp.arange(chunk, dtype=jnp.int32)
    key_pos = jnp.arange(LEN, dtype=jnp.int32)
    cosine, sine = rope_tables(query_pos, HEAD)
    cosine = cosine[None, :, None, :]
    sine = sine[None, :, None, :]
    query_piece = piece_of(query_pos[None, :, None], starts[:, None, :])
    key_piece = piece_of(key_pos[None, :, None], starts[:, None, :])
    before = key_pos[None, None, :] <= query_pos[None, :, None]
    same = (query_piece[:, :, None] > 0) & (query_piece[:, :, None] == key_piece[:, None, :])
    allowed_pairs = before | same

    query_rot = apply_rope(
        projected[:, :query_cols].reshape(seqs, chunk, query_heads, HEAD), cosine, sine
    ).astype(jnp.bfloat16)
    key_rot = apply_rope(
        projected[:, query_cols : query_cols + key_cols].reshape(seqs, chunk, own_keys, HEAD),
        cosine,
        sine,
    ).astype(jnp.bfloat16)
    value_own = projected[:, query_cols + key_cols :].astype(jnp.bfloat16)
    key_local = jnp.concatenate(
        [key_rot.reshape(seqs, chunk, key_cols), value_own.reshape(seqs, chunk, key_cols)], axis=2
    )
    key_all = line_gather(key_local, 1)

    query_split = query_rot.reshape(seqs, chunk, own_keys, kv_group, HEAD)
    query_split = query_split.transpose(0, 2, 1, 3, 4).reshape(-1, chunk, kv_group, HEAD)

    def split_keys(values):
        values = values.reshape(seqs, LEN, own_keys, HEAD)
        return values.transpose(0, 2, 1, 3).reshape(-1, LEN, HEAD)

    key_split = split_keys(key_all[:, :, :key_cols])
    value_split = split_keys(key_all[:, :, key_cols:])
    pairs = jnp.repeat(allowed_pairs, own_keys, axis=0)
    mixed, log_totals = lax.map(
        lambda p: head_forward(p[0], p[1], p[2], p[3]),
        (query_split, key_split, value_split, pairs),
    )

    def join_heads(values):
        values = values.reshape(seqs, own_keys, chunk, kv_group, HEAD).transpose(0, 2, 1, 3, 4)
        return values.reshape(rows, query_cols)

    def split_heads(values):
        values = values.reshape(seqs, chunk, own_keys, kv_group, HEAD).transpose(0, 2, 1, 3, 4)
        return values.reshape(-1, chunk, kv_group, HEAD)

    attn_out = join_heads(mixed).astype(jnp.bfloat16)
    hidden_one = stream + branch_scale * plane_scatter(attn_out, attn_back, False)
    inverse_two, normed_two = norm_forward(hidden_one, gain_two)
    normed_two_all = plane_gather(normed_two)
    gate_up = product(normed_two_all, ffn_in, False)
    gate_val = gate_up[:, :hidden]
    up_val = gate_up[:, hidden:]
    sigma = jax.nn.sigmoid(gate_val)
    silu_gate = gate_val * sigma
    hidden_units = (silu_gate * up_val).astype(jnp.bfloat16)
    hidden_two = hidden_one + branch_scale * plane_scatter(hidden_units, ffn_back, False)
    output = to_tiles(hidden_two.astype(jnp.bfloat16))

    branch_two = (branch_scale * grad_two).astype(jnp.bfloat16)
    branch_two_all = plane_gather(branch_two)
    grad_down = outer_sum(hidden_units, branch_two_all)
    grad_hidden = product(branch_two_all, ffn_back, True)
    grad_gate_val = (grad_hidden * up_val * sigma * (1.0 + gate_val * (1.0 - sigma))).astype(
        jnp.bfloat16
    )
    grad_up_val = (grad_hidden * silu_gate).astype(jnp.bfloat16)
    grad_gate_up = jnp.concatenate([grad_gate_val, grad_up_val], axis=1)
    grad_ffn_in = outer_sum(normed_two_all, grad_gate_up)
    grad_normed_two = plane_scatter(grad_gate_up, ffn_in, True)
    grad_stream_two, grad_norm2 = norm_backward(hidden_one, inverse_two, gain_two, grad_normed_two)
    grad_one = grad_two + grad_stream_two
    branch_one_all = plane_gather((branch_scale * grad_one).astype(jnp.bfloat16))
    grad_out = outer_sum(attn_out, branch_one_all)
    grad_attn = split_heads(product(branch_one_all, attn_back, True).astype(jnp.bfloat16))
    grad_q, grad_k, grad_v = lax.map(
        lambda p: head_backward(p[0], p[1], p[2], p[3], p[4], p[5]),
        (query_split, key_split, value_split, grad_attn, log_totals, pairs),
    )

    def join_keys(values):
        values = values.reshape(seqs, own_keys, LEN, HEAD).transpose(0, 2, 1, 3)
        return values.reshape(seqs, LEN, key_cols)

    key_terms = jnp.concatenate([join_keys(grad_k), join_keys(grad_v)], axis=2)
    key_owned = line_scatter(key_terms, 1).astype(jnp.float32)
    grad_q_pre = rope_back(
        join_heads(grad_q).reshape(seqs, chunk, query_heads, HEAD), cosine, sine
    )
    grad_k_pre = rope_back(
        key_owned[:, :, :key_cols].reshape(seqs, chunk, own_keys, HEAD), cosine, sine
    )
    grad_projected = jnp.concatenate(
        [
            grad_q_pre.reshape(rows, query_cols),
            grad_k_pre.reshape(rows, key_cols),
            key_owned[:, :, key_cols:].reshape(rows, key_cols),
        ],
        axis=1,
    ).astype(jnp.bfloat16)
    grad_attn_in = outer_sum(normed_one_all, grad_projected)
    grad_normed_one = plane_scatter(grad_projected, attn_in, True)
    grad_stream_one, grad_norm1 = norm_backward(stream, inverse_one, gain_one, grad_normed_one)
    input_grad = to_tiles((grad_one + grad_stream_one).astype(jnp.bfloat16))

    def spread_cols(own):
        return lax.all_gather(own, "dp", axis=1, tiled=True).astype(jnp.float32)

    def spread_rows(own):
        return lax.all_gather(own, "dp", axis=0, tiled=True).astype(jnp.float32)

    def spread_keys(own):
        every = lax.all_gather(own, "dp", axis=0).astype(jnp.float32)
        every = every.reshape(dp_count // share, share, -1, key_cols).sum(axis=1)
        return every.transpose(1, 0, 2).reshape(every.shape[1], -1)

    grad_down = spread_rows(line_scatter(grad_down, 1))
    own_ffn = line_scatter(grad_ffn_in, 0)
    grad_gate = spread_cols(own_ffn[:, :hidden])
    grad_up = spread_cols(own_ffn[:, hidden:])
    grad_out = spread_rows(line_scatter(grad_out, 1))
    own_attn = line_scatter(grad_attn_in, 0)
    grad_query = spread_cols(own_attn[:, :query_cols])
    grad_key = spread_keys(own_attn[:, query_cols : query_cols + key_cols])
    grad_value = spread_keys(own_attn[:, query_cols + key_cols :])
    norms = lax.psum(jnp.stack([grad_norm1, grad_norm2]), ("dp", "mx", "my"))
    norms = lax.dynamic_slice_in_dim(norms, mx_index * norm1_gain.shape[0], norm1_gain.shape[0], 1)
    return (
        output,
        input_grad,
        norms[0],
        grad_query,
        grad_key,
        grad_value,
        grad_out,
        norms[1],
        grad_gate,
        grad_up,
        grad_down,
    )


def solution(mesh):
    placed = (
        P(("dp", "my"), "mx"),
        P(("dp", "my"), "mx"),
        P("dp", None),
        P("mx"),
        P("mx", "my"),
        P("mx", "my"),
        P("mx", "my"),
        P("my", "mx"),
        P("mx"),
        P("mx", "my"),
        P("mx", "my"),
        P("my", "mx"),
    )
    return jax.shard_map(
        shards,
        mesh=mesh,
        in_specs=placed,
        out_specs=(
            P(("dp", "my"), "mx"),
            P(("dp", "my"), "mx"),
            P("mx"),
            P("mx", "my"),
            P("mx", "my"),
            P("mx", "my"),
            P("my", "mx"),
            P("mx"),
            P("mx", "my"),
            P("mx", "my"),
            P("my", "mx"),
        ),
        check_vma=False,
    )
```

```python
import functools

import jax
import jax.numpy as jnp
from jax import lax
from jax.experimental import pallas as pl
from jax.experimental.pallas import tpu as pltpu
from jax.sharding import PartitionSpec as P

D = 2048
HEAD = 64
LEN = 1024
PIECE = 256


epsilon = 1e-05
rope_base = 10000000.0
branch_scale = 0.22
score_scale = 0.015625
masked_score = -1e30


def rope_tables(positions, head_width):
    half_width = head_width // 2
    steps_idx = jnp.arange(half_width, dtype=jnp.float32)
    freqs = jnp.exp(-jnp.log(jnp.float32(rope_base)) * 2.0 * steps_idx / head_width)
    angles = positions.astype(jnp.float32)[:, None] * freqs[None, :]
    cosine = jnp.cos(angles)
    sine = jnp.sin(angles)
    return (jnp.concatenate([cosine, cosine], 1), jnp.concatenate([sine, sine], 1))


def rotate_half(values):
    half_width = values.shape[-1] // 2
    return jnp.concatenate([-values[..., half_width:], values[..., :half_width]], -1)


def apply_rope(values, cosine, sine):
    return values * cosine + rotate_half(values) * sine


def rope_back(values, cosine, sine):
    return values * cosine - rotate_half(values) * sine


def product(left, weight, flipped):
    if flipped:
        return lax.dot_general(
            left, weight, (((1,), (1,)), ((), ())), preferred_element_type=jnp.float32
        )
    return jnp.dot(left, weight, preferred_element_type=jnp.float32)


def outer_sum(left, right):
    return lax.dot_general(
        left, right, (((0,), (0,)), ((), ())), preferred_element_type=jnp.float32
    )


def score_bias(starts_ref, offset_ref, seq, chunk, pieces):
    query_pos = offset_ref[0] + lax.broadcasted_iota(jnp.int32, (1, chunk), 1)
    key_pos = lax.broadcasted_iota(jnp.int32, (LEN, 1), 0)
    query_piece = jnp.zeros((1, chunk), jnp.int32)
    key_piece = jnp.full((LEN, 1), -1, jnp.int32)
    for p in range(pieces):
        begin = starts_ref[seq * pieces + p]
        inside = (query_pos >= begin) & (query_pos < begin + PIECE)
        query_piece = jnp.where(inside, p + 1, query_piece)
        inside = (key_pos >= begin) & (key_pos < begin + PIECE)
        key_piece = jnp.where(inside, p + 1, key_piece)
    seen = (key_pos <= query_pos) | (key_piece == query_piece)
    return jnp.where(seen, 0.0, masked_score).astype(jnp.float32)


def dot_rows(left, right):
    return jnp.dot(left, right, preferred_element_type=jnp.float32)


def attend_kernel(starts_ref, offset_ref, query_ref, key_ref, value_ref, out_ref, total_ref, *, own_keys, group, pieces):
    chunk = query_ref.shape[2] // group
    bias = score_bias(starts_ref, offset_ref, pl.program_id(0) // own_keys, chunk, pieces)
    key = key_ref[0]
    value = value_ref[0]
    for g in range(group):
        at = slice(g * chunk, (g + 1) * chunk)
        scores = dot_rows(key, query_ref[0, :, at]) * score_scale + bias
        top = jnp.max(scores, axis=0, keepdims=True)
        shifted = jnp.exp(scores - top)
        total = jnp.sum(shifted, axis=0, keepdims=True)
        probs = (shifted * (1.0 / total)).astype(jnp.bfloat16)
        out_ref[0, :, at] = dot_rows(value, probs).astype(jnp.bfloat16)
        total_ref[0, :, at] = top + jnp.log(total)


def attend_back_kernel(
    starts_ref, offset_ref, query_ref, rows_ref, key_ref, value_ref, keyt_ref, grad_ref,
    grad_rows_ref, total_ref, dq_ref, dk_ref, dv_ref, *, own_keys, group, pieces
):
    chunk = query_ref.shape[2] // group
    bias = score_bias(starts_ref, offset_ref, pl.program_id(0) // own_keys, chunk, pieces)
    key = key_ref[0]
    value = value_ref[0]
    keyt = keyt_ref[0]
    grad_key = jnp.zeros(key.shape, jnp.float32)
    grad_value = jnp.zeros(key.shape, jnp.float32)
    for g in range(group):
        at = slice(g * chunk, (g + 1) * chunk)
        scores = dot_rows(key, query_ref[0, :, at]) * score_scale + bias
        probs = jnp.exp(scores - total_ref[0, :, at])
        grad_probs = dot_rows(value, grad_ref[0, :, at])
        scaled = probs * grad_probs
        row_dot = jnp.sum(scaled, axis=0, keepdims=True)
        grad_scores = (scaled - probs * row_dot).astype(jnp.bfloat16)
        dq_ref[0, :, at] = dot_rows(keyt, grad_scores) * score_scale
        grad_key = grad_key + dot_rows(grad_scores, rows_ref[0, at, :])
        grad_value = grad_value + dot_rows(probs.astype(jnp.bfloat16), grad_rows_ref[0, at, :])
    dk_ref[0] = (grad_key * score_scale).astype(jnp.bfloat16)
    dv_ref[0] = grad_value.astype(jnp.bfloat16)


def whole_block(array):
    return pl.BlockSpec((1,) + array.shape[1:], lambda i: (i, 0, 0))


def attend_call(kernel, starts, offset, arrays, outs, own_keys, group, flops):
    smem = pl.BlockSpec(memory_space=pltpu.SMEM)
    return pl.pallas_call(
        functools.partial(kernel, own_keys=own_keys, group=group, pieces=starts.shape[-1]),
        grid=(arrays[0].shape[0],),
        in_specs=[smem, smem] + [whole_block(a) for a in arrays],
        out_specs=[whole_block(o) for o in outs],
        out_shape=outs,
        cost_estimate=pl.CostEstimate(flops=flops, transcendentals=0, bytes_accessed=0),
    )(starts.reshape(-1), offset.reshape(1), *arrays)


PLANE = ("dp", "my")


def swap(values, bit):
    count = lax.axis_size("dp")
    return lax.ppermute(values, "dp", [(i, i ^ bit) for i in range(count)])


def swap_core(values):
    count = lax.axis_size("my")
    return lax.ppermute(values, "my", [(i, i ^ 1) for i in range(count)])


def small_plane():
    return lax.axis_size("dp") == 4 and lax.axis_size("my") == 2


def plane_gather(values):
    if not small_plane():
        return lax.all_gather(values, PLANE, axis=0, tiled=True)
    half = values.shape[0] // 2
    from_x = swap(values, 1)
    from_y = swap(values, 2)
    core_own = swap_core(values)
    corner_low = swap(from_y[:half], 1)
    corner_high = swap(from_x[half:], 2)
    core_x = swap_core(from_x)
    core_y = swap_core(from_y)
    corner = jnp.concatenate([corner_low, corner_high], axis=0)
    core_corner = swap_core(corner)
    return jnp.concatenate(
        [values, from_x, from_y, corner, core_own, core_x, core_y, core_corner], axis=0
    )


def plane_scatter(left, weight, flipped):
    if not small_plane():
        return lax.psum_scatter(
            product(left, weight, flipped).astype(jnp.bfloat16),
            PLANE,
            scatter_dimension=0,
            tiled=True,
        ).astype(jnp.float32)
    rows = left.shape[0] // 8
    half = rows // 2
    low = jnp.bfloat16
    wide = jnp.float32
    other = product(left[4 * rows :], weight, flipped).astype(low)
    got = [swap_core(other[k * rows : (k + 1) * rows]) for k in range(4)]
    own = product(left[: 4 * rows], weight, flipped).astype(low)
    part = [
        own[k * rows : (k + 1) * rows].astype(wide) + got[k].astype(wide) for k in range(4)
    ]
    via_x = swap(jnp.concatenate([part[3][:half], part[1][:half]], 0).astype(low), 1).astype(wide)
    via_y = swap(jnp.concatenate([part[3][half:], part[2][half:]], 0).astype(low), 2).astype(wide)
    next_y = swap((part[2][:half] + via_x[:half]).astype(low), 2)
    next_x = swap((part[1][half:] + via_y[:half]).astype(low), 1)
    first = part[0][:half] + via_x[half:] + next_y.astype(wide)
    second = part[0][half:] + via_y[half:] + next_x.astype(wide)
    return jnp.concatenate([first, second], axis=0)


def plane_starts(starts):
    if not small_plane():
        return lax.all_gather(starts, "dp", axis=0, tiled=True)
    from_x = swap(starts, 1)
    from_y = swap(starts, 2)
    every = jnp.stack([starts, from_x, from_y, swap(from_y, 1)])
    my_index = lax.axis_index("my")
    return jnp.concatenate([every[:, my_index], every[:, my_index ^ 1]], axis=0)


def plane_sum(values):
    if not small_plane():
        return lax.psum(values, PLANE)
    values = values + swap_core(values)
    values = values + swap(values, 1)
    return values + swap(values, 2)


def dp_blocks(own):
    index = lax.axis_index("dp")
    if not small_plane():
        every = lax.all_gather(own, "dp", axis=0)
        return [(k, every[k]) for k in range(every.shape[0])]
    half = own.shape[0] // 2
    from_x = swap(own, 1)
    from_y = swap(own, 2)
    corner_low = swap(from_y[:half], 1)
    corner_high = swap(from_x[half:], 2)
    corner = jnp.concatenate([corner_low, corner_high], axis=0)
    return [(index ^ k, b) for k, b in enumerate([own, from_x, from_y, corner])]


def spread(own, axis):
    shape = list(own.shape)
    shape[axis] *= lax.axis_size("dp")
    result = jnp.zeros(shape, jnp.float32)
    for index, block in dp_blocks(own):
        result = lax.dynamic_update_slice_in_dim(
            result, block.astype(jnp.float32), index * own.shape[axis], axis
        )
    return result


def tie(value, *after):
    return lax.optimization_barrier((value,) + after)


def line_exchange(blocks):
    count = lax.axis_size("mx")
    index = lax.axis_index("mx")

    def at(offset):
        return lax.dynamic_index_in_dim(blocks, (index + offset) % count, 0, keepdims=False)

    result = jnp.zeros_like(blocks)
    result = lax.dynamic_update_index_in_dim(result, at(0), index, 0)
    for shift in range(1, count):
        moved = lax.ppermute(at(shift), "mx", [(i, (i + shift) % count) for i in range(count)])
        result = lax.dynamic_update_index_in_dim(result, moved, (index - shift) % count, 0)
    return result


def to_rows(values):
    count = lax.axis_size("mx")
    blocks = line_exchange(values.reshape(count, -1, values.shape[1]))
    return blocks.transpose(1, 0, 2).reshape(blocks.shape[1], -1)


def to_tiles(values):
    count = lax.axis_size("mx")
    blocks = values.reshape(values.shape[0], count, -1).transpose(1, 0, 2)
    return line_exchange(blocks).reshape(-1, blocks.shape[2])


def line_gather(values, axis):
    return lax.all_gather(values, "mx", axis=axis, tiled=True)


def line_scatter(values, axis):
    return lax.psum_scatter(
        values.astype(jnp.bfloat16), "mx", scatter_dimension=axis, tiled=True
    )


def norm_forward(stream, gain):
    mean = jnp.mean(stream * stream, axis=1, keepdims=True)
    inverse = lax.rsqrt(mean + epsilon)
    return (inverse, (stream * inverse * gain[None, :]).astype(jnp.bfloat16))


def norm_backward(stream, inverse, gain, grad_normed):
    scaled = gain[None, :] * grad_normed
    row_mean = jnp.mean(stream * scaled, axis=1, keepdims=True)
    grad_stream = inverse * scaled - stream * inverse * inverse * inverse * row_mean
    grad_gain = jnp.sum(grad_normed * stream * inverse, axis=0)
    return (grad_stream, grad_gain)


def shards(
    tokens,
    output_grad,
    picture_starts,
    norm1_gain,
    query_weight,
    key_weight,
    value_weight,
    out_weight,
    norm2_gain,
    gate_weight,
    up_weight,
    down_weight,
):
    mx_count = lax.axis_size("mx")
    dp_count = lax.axis_size("dp")
    dp_index = lax.axis_index("dp")
    mx_index = lax.axis_index("mx")
    chunk = LEN // mx_count
    seqs = dp_count * lax.axis_size("my")
    rows = seqs * chunk
    query_cols = query_weight.shape[1] // dp_count
    query_heads = query_cols // HEAD
    key_heads = key_weight.shape[1] // HEAD
    share = max(1, dp_count // key_heads)
    key_cols = key_weight.shape[1] * share // dp_count
    own_keys = key_cols // HEAD
    kv_group = query_heads // own_keys
    hidden = gate_weight.shape[1] // dp_count

    def cols(weight, width, index):
        return lax.dynamic_slice_in_dim(weight, index * width, width, axis=1)

    def rows_of(weight, width):
        return lax.dynamic_slice_in_dim(weight, dp_index * width, width, axis=0)

    key_index = dp_index // share
    attn_in = line_gather(
        jnp.concatenate(
            [
                cols(query_weight, query_cols, dp_index),
                cols(key_weight, key_cols, key_index),
                cols(value_weight, key_cols, key_index),
            ],
            axis=1,
        ),
        0,
    )
    attn_back = line_gather(rows_of(out_weight, query_cols), 1)
    gains = jnp.stack([norm1_gain, norm2_gain])
    gains = line_exchange(jnp.broadcast_to(gains, (mx_count,) + gains.shape))
    gain_one, gain_two = gains.transpose(1, 0, 2).reshape(2, -1)
    starts = plane_starts(picture_starts)

    stream = to_rows(tokens).astype(jnp.float32)
    inverse_one, normed_one = norm_forward(stream, gain_one)
    normed_one_all = plane_gather(normed_one)
    projected = product(normed_one_all, attn_in, False)

    query_pos = mx_index * chunk + jnp.arange(chunk, dtype=jnp.int32)
    cosine, sine = rope_tables(query_pos, HEAD)
    cosine = cosine[None, :, None, :]
    sine = sine[None, :, None, :]
    query_rot = apply_rope(
        projected[:, :query_cols].reshape(seqs, chunk, query_heads, HEAD), cosine, sine
    ).astype(jnp.bfloat16)
    key_rot = apply_rope(
        projected[:, query_cols : query_cols + key_cols].reshape(seqs, chunk, own_keys, HEAD),
        cosine,
        sine,
    ).astype(jnp.bfloat16)
    value_own = projected[:, query_cols + key_cols :].astype(jnp.bfloat16)
    key_local = jnp.concatenate(
        [key_rot.reshape(seqs, chunk, key_cols), value_own.reshape(seqs, chunk, key_cols)], axis=2
    )
    key_all = line_gather(key_local, 1)
    down_rows, stream = tie(rows_of(down_weight, hidden), stream)
    ffn_back = line_gather(down_rows, 1)
    ffn_cols = jnp.concatenate(
        [cols(gate_weight, hidden, dp_index), cols(up_weight, hidden, dp_index)], axis=1
    )
    key_all, ffn_cols, late_grad = tie(key_all, ffn_cols, output_grad)
    ffn_in = line_gather(ffn_cols, 0)
    grad_two = to_rows(late_grad).astype(jnp.float32)

    def head_cols(values):
        values = values.reshape(seqs, chunk, own_keys, kv_group, HEAD).transpose(0, 2, 4, 3, 1)
        return values.reshape(-1, HEAD, kv_group * chunk)

    def head_rows(values):
        values = values.reshape(seqs, chunk, own_keys, kv_group, HEAD).transpose(0, 2, 3, 1, 4)
        return values.reshape(-1, kv_group * chunk, HEAD)

    def join_heads(values):
        values = values.reshape(seqs, own_keys, HEAD, kv_group, chunk).transpose(0, 4, 1, 3, 2)
        return values.reshape(rows, query_cols)

    def split_keys(values):
        values = values.reshape(seqs, LEN, own_keys, HEAD)
        return values.transpose(0, 2, 1, 3).reshape(-1, LEN, HEAD)

    query_split = head_cols(query_rot)
    key_split = split_keys(key_all[:, :, :key_cols])
    value_split = split_keys(key_all[:, :, key_cols:])
    offset = mx_index * chunk
    work = 2 * seqs * chunk * query_cols * LEN
    mixed, log_totals = attend_call(
        attend_kernel,
        starts,
        offset,
        [query_split, key_split, value_split.transpose(0, 2, 1)],
        [
            jax.ShapeDtypeStruct(query_split.shape, jnp.bfloat16),
            jax.ShapeDtypeStruct((query_split.shape[0], 1, query_split.shape[2]), jnp.float32),
        ],
        own_keys,
        kv_group,
        2 * work,
    )
    attn_out = join_heads(mixed)
    hidden_one = stream + branch_scale * plane_scatter(attn_out, attn_back, False)
    inverse_two, normed_two = norm_forward(hidden_one, gain_two)
    normed_two_all = plane_gather(normed_two)
    gate_up = product(normed_two_all, ffn_in, False)
    gate_val = gate_up[:, :hidden]
    up_val = gate_up[:, hidden:]
    sigma = jax.nn.sigmoid(gate_val)
    silu_gate = gate_val * sigma
    hidden_units = (silu_gate * up_val).astype(jnp.bfloat16)
    hidden_two = hidden_one + branch_scale * plane_scatter(hidden_units, ffn_back, False)
    output = to_tiles(hidden_two.astype(jnp.bfloat16))

    branch_two = (branch_scale * grad_two).astype(jnp.bfloat16)
    branch_two_all = plane_gather(branch_two)
    grad_down = outer_sum(hidden_units, branch_two_all)
    grad_hidden = product(branch_two_all, ffn_back, True)
    grad_gate_val = (grad_hidden * up_val * sigma * (1.0 + gate_val * (1.0 - sigma))).astype(
        jnp.bfloat16
    )
    grad_up_val = (grad_hidden * silu_gate).astype(jnp.bfloat16)
    grad_gate_up = jnp.concatenate([grad_gate_val, grad_up_val], axis=1)
    grad_normed_two = plane_scatter(grad_gate_up, ffn_in, True)
    own_down = line_scatter(grad_down, 1)
    own_gate = line_scatter(outer_sum(normed_two_all, grad_gate_val), 0)
    own_up = line_scatter(outer_sum(normed_two_all, grad_up_val), 0)
    grad_stream_two, grad_norm2 = norm_backward(hidden_one, inverse_two, gain_two, grad_normed_two)
    grad_one = grad_two + grad_stream_two
    branch_one_all = plane_gather((branch_scale * grad_one).astype(jnp.bfloat16))
    branch_one_all, own_down = tie(branch_one_all, own_down)
    grad_attn = product(branch_one_all, attn_back, True).astype(jnp.bfloat16)
    like_key = jax.ShapeDtypeStruct(key_split.shape, jnp.bfloat16)
    grad_q, grad_k, grad_v = attend_call(
        attend_back_kernel,
        starts,
        offset,
        [
            query_split,
            head_rows(query_rot),
            key_split,
            value_split,
            key_split.transpose(0, 2, 1),
            head_cols(grad_attn),
            head_rows(grad_attn),
            log_totals,
        ],
        [jax.ShapeDtypeStruct(query_split.shape, jnp.float32), like_key, like_key],
        own_keys,
        kv_group,
        5 * work,
    )
    grad_out = outer_sum(attn_out, branch_one_all)

    def key_blocks(values):
        values = values.reshape(seqs, own_keys, mx_count, chunk, HEAD).transpose(2, 0, 3, 1, 4)
        return values.reshape(mx_count, seqs, chunk, key_cols)

    key_terms = jnp.concatenate([key_blocks(grad_k), key_blocks(grad_v)], axis=3)
    key_owned = jnp.sum(line_exchange(key_terms).astype(jnp.float32), axis=0)
    key_owned, own_gate = tie(key_owned, own_gate)
    grad_q_pre = rope_back(
        join_heads(grad_q).reshape(seqs, chunk, query_heads, HEAD), cosine, sine
    )
    grad_k_pre = rope_back(
        key_owned[:, :, :key_cols].reshape(seqs, chunk, own_keys, HEAD), cosine, sine
    )
    grad_projected = jnp.concatenate(
        [
            grad_q_pre.reshape(rows, query_cols),
            grad_k_pre.reshape(rows, key_cols),
            key_owned[:, :, key_cols:].reshape(rows, key_cols),
        ],
        axis=1,
    ).astype(jnp.bfloat16)
    grad_attn_in = outer_sum(normed_one_all, grad_projected)
    grad_normed_one = plane_scatter(grad_projected, attn_in, True)
    grad_normed_one, own_up = tie(grad_normed_one, own_up)
    grad_stream_one, grad_norm1 = norm_backward(stream, inverse_one, gain_one, grad_normed_one)
    input_grad = to_tiles((grad_one + grad_stream_one).astype(jnp.bfloat16))

    def spread_keys(own):
        if share == 1:
            return spread(own, 1)
        every = lax.all_gather(own, "dp", axis=0).astype(jnp.float32)
        every = every.reshape(dp_count // share, share, -1, key_cols).sum(axis=1)
        return every.transpose(1, 0, 2).reshape(every.shape[1], -1)

    def own_norm(total):
        blocks = line_exchange(total.reshape(mx_count, -1))
        return plane_sum(jnp.sum(blocks, axis=0))

    grad_down = spread(own_down, 0)
    grad_gate = spread(own_gate, 1)
    grad_up = spread(own_up, 1)
    grad_out = spread(line_scatter(grad_out, 1), 0)
    own_attn = line_scatter(grad_attn_in, 0)
    grad_query = spread(own_attn[:, :query_cols], 1)
    grad_key = spread_keys(own_attn[:, query_cols : query_cols + key_cols])
    grad_value = spread_keys(own_attn[:, query_cols + key_cols :])
    grad_norm2 = own_norm(grad_norm2)
    grad_norm1 = own_norm(grad_norm1)
    return (
        output,
        input_grad,
        grad_norm1,
        grad_query,
        grad_key,
        grad_value,
        grad_out,
        grad_norm2,
        grad_gate,
        grad_up,
        grad_down,
    )


def solution(mesh):
    placed = (
        P(("dp", "my"), "mx"),
        P(("dp", "my"), "mx"),
        P("dp", None),
        P("mx"),
        P("mx", "my"),
        P("mx", "my"),
        P("mx", "my"),
        P("my", "mx"),
        P("mx"),
        P("mx", "my"),
        P("mx", "my"),
        P("my", "mx"),
    )
    return jax.shard_map(
        shards,
        mesh=mesh,
        in_specs=placed,
        out_specs=(
            P(("dp", "my"), "mx"),
            P(("dp", "my"), "mx"),
            P("mx"),
            P("mx", "my"),
            P("mx", "my"),
            P("mx", "my"),
            P("my", "mx"),
            P("mx"),
            P("mx", "my"),
            P("mx", "my"),
            P("my", "mx"),
        ),
        check_vma=False,
    )
```

```python
import functools

import jax
import jax.numpy as jnp
from jax import lax
from jax.experimental import pallas as pl
from jax.experimental.pallas import tpu as pltpu
from jax.sharding import PartitionSpec as P

D = 2048
HEAD = 64
LEN = 1024
PIECE = 256


epsilon = 1e-05
rope_base = 10000000.0
branch_scale = 0.22
score_scale = 0.015625
masked_score = -1e30


def rope_tables(positions, head_width):
    half_width = head_width // 2
    steps_idx = jnp.arange(half_width, dtype=jnp.float32)
    freqs = jnp.exp(-jnp.log(jnp.float32(rope_base)) * 2.0 * steps_idx / head_width)
    angles = positions.astype(jnp.float32)[:, None] * freqs[None, :]
    cosine = jnp.cos(angles)
    sine = jnp.sin(angles)
    return (jnp.concatenate([cosine, cosine], 1), jnp.concatenate([sine, sine], 1))


def rotate_half(values):
    half_width = values.shape[-1] // 2
    return jnp.concatenate([-values[..., half_width:], values[..., :half_width]], -1)


def apply_rope(values, cosine, sine):
    return values * cosine + rotate_half(values) * sine


def rope_back(values, cosine, sine):
    return values * cosine - rotate_half(values) * sine


def product(left, weight, flipped):
    if flipped:
        return lax.dot_general(
            left, weight, (((1,), (1,)), ((), ())), preferred_element_type=jnp.float32
        )
    return jnp.dot(left, weight, preferred_element_type=jnp.float32)


def outer_sum(left, right):
    return lax.dot_general(
        left, right, (((0,), (0,)), ((), ())), preferred_element_type=jnp.float32
    )


def score_bias(starts_ref, offset_ref, seq, chunk, pieces):
    query_pos = offset_ref[0] + lax.broadcasted_iota(jnp.int32, (1, chunk), 1)
    key_pos = lax.broadcasted_iota(jnp.int32, (LEN, 1), 0)
    query_piece = jnp.zeros((1, chunk), jnp.int32)
    key_piece = jnp.full((LEN, 1), -1, jnp.int32)
    for p in range(pieces):
        begin = starts_ref[seq * pieces + p]
        inside = (query_pos >= begin) & (query_pos < begin + PIECE)
        query_piece = jnp.where(inside, p + 1, query_piece)
        inside = (key_pos >= begin) & (key_pos < begin + PIECE)
        key_piece = jnp.where(inside, p + 1, key_piece)
    seen = (key_pos <= query_pos) | (key_piece == query_piece)
    return jnp.where(seen, 0.0, masked_score).astype(jnp.float32)


def dot_rows(left, right):
    return jnp.dot(left, right, preferred_element_type=jnp.float32)


def attend_kernel(starts_ref, offset_ref, query_ref, key_ref, value_ref, out_ref, total_ref, *, own_keys, group, pieces):
    chunk = query_ref.shape[2] // group
    bias = score_bias(starts_ref, offset_ref, pl.program_id(0) // own_keys, chunk, pieces)
    key = key_ref[0]
    value = value_ref[0]
    for g in range(group):
        at = slice(g * chunk, (g + 1) * chunk)
        scores = dot_rows(key, query_ref[0, :, at]) * score_scale + bias
        top = jnp.max(scores, axis=0, keepdims=True)
        shifted = jnp.exp(scores - top)
        total = jnp.sum(shifted, axis=0, keepdims=True)
        probs = (shifted * (1.0 / total)).astype(jnp.bfloat16)
        out_ref[0, :, at] = dot_rows(value, probs).astype(jnp.bfloat16)
        total_ref[0, :, at] = top + jnp.log(total)


def attend_back_kernel(
    starts_ref, offset_ref, query_ref, rows_ref, key_ref, value_ref, keyt_ref, grad_ref,
    grad_rows_ref, total_ref, dq_ref, dk_ref, dv_ref, *, own_keys, group, pieces
):
    chunk = query_ref.shape[2] // group
    bias = score_bias(starts_ref, offset_ref, pl.program_id(0) // own_keys, chunk, pieces)
    key = key_ref[0]
    value = value_ref[0]
    keyt = keyt_ref[0]
    grad_key = jnp.zeros(key.shape, jnp.float32)
    grad_value = jnp.zeros(key.shape, jnp.float32)
    for g in range(group):
        at = slice(g * chunk, (g + 1) * chunk)
        scores = dot_rows(key, query_ref[0, :, at]) * score_scale + bias
        probs = jnp.exp(scores - total_ref[0, :, at])
        grad_probs = dot_rows(value, grad_ref[0, :, at])
        scaled = probs * grad_probs
        row_dot = jnp.sum(scaled, axis=0, keepdims=True)
        grad_scores = (scaled - probs * row_dot).astype(jnp.bfloat16)
        dq_ref[0, :, at] = dot_rows(keyt, grad_scores) * score_scale
        grad_key = grad_key + dot_rows(grad_scores, rows_ref[0, at, :])
        grad_value = grad_value + dot_rows(probs.astype(jnp.bfloat16), grad_rows_ref[0, at, :])
    dk_ref[0] = (grad_key * score_scale).astype(jnp.bfloat16)
    dv_ref[0] = grad_value.astype(jnp.bfloat16)


def whole_block(array):
    return pl.BlockSpec((1,) + array.shape[1:], lambda i: (i, 0, 0))


def attend_call(kernel, starts, offset, arrays, outs, own_keys, group, flops):
    smem = pl.BlockSpec(memory_space=pltpu.SMEM)
    return pl.pallas_call(
        functools.partial(kernel, own_keys=own_keys, group=group, pieces=starts.shape[-1]),
        grid=(arrays[0].shape[0],),
        in_specs=[smem, smem] + [whole_block(a) for a in arrays],
        out_specs=[whole_block(o) for o in outs],
        out_shape=outs,
        cost_estimate=pl.CostEstimate(flops=flops, transcendentals=0, bytes_accessed=0),
    )(starts.reshape(-1), offset.reshape(1), *arrays)


PLANE = ("dp", "my")


def swap(values, bit):
    count = lax.axis_size("dp")
    return lax.ppermute(values, "dp", [(i, i ^ bit) for i in range(count)])


def swap_core(values):
    count = lax.axis_size("my")
    return lax.ppermute(values, "my", [(i, i ^ 1) for i in range(count)])


def small_plane():
    return lax.axis_size("dp") == 4 and lax.axis_size("my") == 2


def plane_gather(values):
    if not small_plane():
        return lax.all_gather(values, PLANE, axis=0, tiled=True)
    half = values.shape[0] // 2
    from_x = swap(values, 1)
    from_y = swap(values, 2)
    core_own = swap_core(values)
    corner_low = swap(from_y[:half], 1)
    corner_high = swap(from_x[half:], 2)
    core_x = swap_core(from_x)
    core_y = swap_core(from_y)
    corner = jnp.concatenate([corner_low, corner_high], axis=0)
    core_corner = swap_core(corner)
    return jnp.concatenate(
        [values, from_x, from_y, corner, core_own, core_x, core_y, core_corner], axis=0
    )


def plane_products(left, weight, flipped):
    if not small_plane():
        return (product(left, weight, flipped).astype(jnp.bfloat16),)
    middle = left.shape[0] // 2
    other = product(left[middle:], weight, flipped).astype(jnp.bfloat16)
    return (other, product(left[:middle], weight, flipped).astype(jnp.bfloat16))


def plane_scatter(left, weight, flipped):
    return plane_reduce(*plane_products(left, weight, flipped))


def plane_reduce(*products):
    if not small_plane():
        return lax.psum_scatter(
            products[0],
            PLANE,
            scatter_dimension=0,
            tiled=True,
        ).astype(jnp.float32)
    other, own = products
    rows = own.shape[0] // 4
    half = rows // 2
    low = jnp.bfloat16
    wide = jnp.float32
    got = [swap_core(other[k * rows : (k + 1) * rows]) for k in range(4)]
    part = [
        own[k * rows : (k + 1) * rows].astype(wide) + got[k].astype(wide) for k in range(4)
    ]
    via_x = swap(jnp.concatenate([part[3][:half], part[1][:half]], 0).astype(low), 1).astype(wide)
    via_y = swap(jnp.concatenate([part[3][half:], part[2][half:]], 0).astype(low), 2).astype(wide)
    next_y = swap((part[2][:half] + via_x[:half]).astype(low), 2)
    next_x = swap((part[1][half:] + via_y[:half]).astype(low), 1)
    first = part[0][:half] + via_x[half:] + next_y.astype(wide)
    second = part[0][half:] + via_y[half:] + next_x.astype(wide)
    return jnp.concatenate([first, second], axis=0)


def plane_starts(starts):
    if not small_plane():
        return lax.all_gather(starts, "dp", axis=0, tiled=True)
    from_x = swap(starts, 1)
    from_y = swap(starts, 2)
    every = jnp.stack([starts, from_x, from_y, swap(from_y, 1)])
    my_index = lax.axis_index("my")
    return jnp.concatenate([every[:, my_index], every[:, my_index ^ 1]], axis=0)


def plane_sum(values):
    if not small_plane():
        return lax.psum(values, PLANE)
    values = values + swap_core(values)
    values = values + swap(values, 1)
    return values + swap(values, 2)


def dp_blocks(own):
    index = lax.axis_index("dp")
    if not small_plane():
        every = lax.all_gather(own, "dp", axis=0)
        return [(k, every[k]) for k in range(every.shape[0])]
    half = own.shape[0] // 2
    from_x = swap(own, 1)
    from_y = swap(own, 2)
    corner_low = swap(from_y[:half], 1)
    corner_high = swap(from_x[half:], 2)
    corner = jnp.concatenate([corner_low, corner_high], axis=0)
    return [(index ^ k, b) for k, b in enumerate([own, from_x, from_y, corner])]


def spread(own, axis):
    shape = list(own.shape)
    shape[axis] *= lax.axis_size("dp")
    result = jnp.zeros(shape, jnp.float32)
    for index, block in dp_blocks(own):
        result = lax.dynamic_update_slice_in_dim(
            result, block.astype(jnp.float32), index * own.shape[axis], axis
        )
    return result


def tie(value, *after):
    return lax.optimization_barrier((value,) + after)


def line_send(blocks):
    count = lax.axis_size("mx")
    index = lax.axis_index("mx")

    def at(offset):
        return lax.dynamic_index_in_dim(blocks, (index + offset) % count, 0, keepdims=False)

    return [at(0)] + [
        lax.ppermute(at(shift), "mx", [(i, (i + shift) % count) for i in range(count)])
        for shift in range(1, count)
    ]


def line_place(received):
    count = len(received)
    index = lax.axis_index("mx")
    placed = []
    for place in range(count):
        turn = (index - place) % count
        block = received[0]
        for r in range(1, count):
            block = jnp.where(turn == r, received[r], block)
        placed.append(block)
    return placed


def line_sum(received):
    total = received[0].astype(jnp.float32)
    for block in received[1:]:
        total = total + block.astype(jnp.float32)
    return total


def to_rows(values):
    count = lax.axis_size("mx")
    blocks = line_send(values.reshape(count, -1, values.shape[1]))
    return jnp.concatenate(line_place(blocks), axis=1)


def send_tiles(values):
    count = lax.axis_size("mx")
    return line_send(values.reshape(values.shape[0], count, -1).transpose(1, 0, 2))


def place_tiles(received):
    return jnp.concatenate(line_place(received), axis=0)


def line_gather(values, axis):
    return lax.all_gather(values, "mx", axis=axis, tiled=True)


def line_scatter(values, axis):
    return lax.psum_scatter(
        values.astype(jnp.bfloat16), "mx", scatter_dimension=axis, tiled=True
    )


def norm_forward(stream, gain):
    mean = jnp.mean(stream * stream, axis=1, keepdims=True)
    inverse = lax.rsqrt(mean + epsilon)
    return (inverse, (stream * inverse * gain[None, :]).astype(jnp.bfloat16))


def norm_backward(stream, inverse, gain, grad_normed):
    scaled = gain[None, :] * grad_normed
    row_mean = jnp.mean(stream * scaled, axis=1, keepdims=True)
    grad_stream = inverse * scaled - stream * inverse * inverse * inverse * row_mean
    grad_gain = jnp.sum(grad_normed * stream * inverse, axis=0)
    return (grad_stream, grad_gain)


def shards(
    tokens,
    output_grad,
    picture_starts,
    norm1_gain,
    query_weight,
    key_weight,
    value_weight,
    out_weight,
    norm2_gain,
    gate_weight,
    up_weight,
    down_weight,
):
    mx_count = lax.axis_size("mx")
    dp_count = lax.axis_size("dp")
    dp_index = lax.axis_index("dp")
    mx_index = lax.axis_index("mx")
    chunk = LEN // mx_count
    seqs = dp_count * lax.axis_size("my")
    rows = seqs * chunk
    query_cols = query_weight.shape[1] // dp_count
    query_heads = query_cols // HEAD
    key_heads = key_weight.shape[1] // HEAD
    share = max(1, dp_count // key_heads)
    key_cols = key_weight.shape[1] * share // dp_count
    own_keys = key_cols // HEAD
    kv_group = query_heads // own_keys
    hidden = gate_weight.shape[1] // dp_count

    def cols(weight, width, index):
        return lax.dynamic_slice_in_dim(weight, index * width, width, axis=1)

    def rows_of(weight, width):
        return lax.dynamic_slice_in_dim(weight, dp_index * width, width, axis=0)

    key_index = dp_index // share
    attn_cols = query_cols + 2 * key_cols
    attn_all = line_gather(
        jnp.concatenate(
            [
                cols(query_weight, query_cols, dp_index),
                cols(key_weight, key_cols, key_index),
                cols(value_weight, key_cols, key_index),
                rows_of(out_weight, query_cols).T,
            ],
            axis=1,
        ),
        0,
    )
    attn_in = attn_all[:, :attn_cols]
    attn_back = attn_all[:, attn_cols:]
    gains = jnp.stack([norm1_gain, norm2_gain])
    gains = line_place(line_send(jnp.broadcast_to(gains, (mx_count,) + gains.shape)))
    gain_one, gain_two = jnp.concatenate(gains, axis=1)
    starts = plane_starts(picture_starts)

    stream = to_rows(tokens).astype(jnp.float32)
    inverse_one, normed_one = norm_forward(stream, gain_one)
    normed_one_all = plane_gather(normed_one)
    projected = product(normed_one_all, attn_in, False)

    query_pos = mx_index * chunk + jnp.arange(chunk, dtype=jnp.int32)
    cosine, sine = rope_tables(query_pos, HEAD)
    cosine = cosine[None, :, None, :]
    sine = sine[None, :, None, :]
    query_rot = apply_rope(
        projected[:, :query_cols].reshape(seqs, chunk, query_heads, HEAD), cosine, sine
    ).astype(jnp.bfloat16)
    key_rot = apply_rope(
        projected[:, query_cols : query_cols + key_cols].reshape(seqs, chunk, own_keys, HEAD),
        cosine,
        sine,
    ).astype(jnp.bfloat16)
    value_own = projected[:, query_cols + key_cols :].astype(jnp.bfloat16)
    key_local = jnp.concatenate(
        [key_rot.reshape(seqs, chunk, key_cols), value_own.reshape(seqs, chunk, key_cols)], axis=2
    )
    key_all = line_gather(key_local, 1)
    down_rows, stream = tie(rows_of(down_weight, hidden), stream)
    ffn_back = line_gather(down_rows, 1)
    ffn_cols = jnp.concatenate(
        [cols(gate_weight, hidden, dp_index), cols(up_weight, hidden, dp_index)], axis=1
    )
    key_all, ffn_cols, late_grad = tie(key_all, ffn_cols, output_grad)
    ffn_in = line_gather(ffn_cols, 0)
    grad_two = to_rows(late_grad).astype(jnp.float32)

    def head_cols(values):
        values = values.reshape(seqs, chunk, own_keys, kv_group, HEAD).transpose(0, 2, 4, 3, 1)
        return values.reshape(-1, HEAD, kv_group * chunk)

    def head_rows(values):
        values = values.reshape(seqs, chunk, own_keys, kv_group, HEAD).transpose(0, 2, 3, 1, 4)
        return values.reshape(-1, kv_group * chunk, HEAD)

    def join_heads(values):
        values = values.reshape(seqs, own_keys, HEAD, kv_group, chunk).transpose(0, 4, 1, 3, 2)
        return values.reshape(rows, query_cols)

    def split_keys(values):
        values = values.reshape(seqs, LEN, own_keys, HEAD)
        return values.transpose(0, 2, 1, 3).reshape(-1, LEN, HEAD)

    query_split = head_cols(query_rot)
    key_split = split_keys(key_all[:, :, :key_cols])
    value_split = split_keys(key_all[:, :, key_cols:])
    offset = mx_index * chunk
    work = 2 * seqs * chunk * query_cols * LEN
    mixed, log_totals = attend_call(
        attend_kernel,
        starts,
        offset,
        [query_split, key_split, value_split.transpose(0, 2, 1)],
        [
            jax.ShapeDtypeStruct(query_split.shape, jnp.bfloat16),
            jax.ShapeDtypeStruct((query_split.shape[0], 1, query_split.shape[2]), jnp.float32),
        ],
        own_keys,
        kv_group,
        2 * work,
    )
    attn_out = join_heads(mixed)
    hidden_one = stream + branch_scale * plane_scatter(attn_out, attn_back, True)
    inverse_two, normed_two = norm_forward(hidden_one, gain_two)
    normed_two_all = plane_gather(normed_two)
    gate_up = product(normed_two_all, ffn_in, False)
    gate_val = gate_up[:, :hidden]
    up_val = gate_up[:, hidden:]
    sigma = jax.nn.sigmoid(gate_val)
    silu_gate = gate_val * sigma
    hidden_units = (silu_gate * up_val).astype(jnp.bfloat16)
    down_products = plane_products(hidden_units, ffn_back, False)

    branch_two = (branch_scale * grad_two).astype(jnp.bfloat16)
    branch_two_all = plane_gather(branch_two)
    grad_down = outer_sum(hidden_units, branch_two_all)
    grad_hidden = product(branch_two_all, ffn_back, True)
    grad_gate_val = (grad_hidden * up_val * sigma * (1.0 + gate_val * (1.0 - sigma))).astype(
        jnp.bfloat16
    )
    grad_up_val = (grad_hidden * silu_gate).astype(jnp.bfloat16)
    grad_gate_up = jnp.concatenate([grad_gate_val, grad_up_val], axis=1)
    grad_normed_two = plane_scatter(grad_gate_up, ffn_in, True)
    own_down = line_scatter(grad_down, 1)
    own_gate = line_scatter(outer_sum(normed_two_all, grad_gate_val), 0)
    own_up = line_scatter(outer_sum(normed_two_all, grad_up_val), 0)
    grad_stream_two, grad_norm2 = norm_backward(hidden_one, inverse_two, gain_two, grad_normed_two)
    grad_one = grad_two + grad_stream_two
    branch_one_all = plane_gather((branch_scale * grad_one).astype(jnp.bfloat16))
    branch_one_all, own_down, *down_products = tie(branch_one_all, own_down, *down_products)
    hidden_two = hidden_one + branch_scale * plane_reduce(*down_products)
    output_tiles = send_tiles(hidden_two.astype(jnp.bfloat16))
    grad_attn = product(branch_one_all, attn_back, False).astype(jnp.bfloat16)
    like_key = jax.ShapeDtypeStruct(key_split.shape, jnp.bfloat16)
    grad_q, grad_k, grad_v = attend_call(
        attend_back_kernel,
        starts,
        offset,
        [
            query_split,
            head_rows(query_rot),
            key_split,
            value_split,
            key_split.transpose(0, 2, 1),
            head_cols(grad_attn),
            head_rows(grad_attn),
            log_totals,
        ],
        [jax.ShapeDtypeStruct(query_split.shape, jnp.float32), like_key, like_key],
        own_keys,
        kv_group,
        5 * work,
    )
    grad_out = outer_sum(attn_out, branch_one_all)

    def key_blocks(values):
        values = values.reshape(seqs, own_keys, mx_count, chunk, HEAD).transpose(2, 0, 3, 1, 4)
        return values.reshape(mx_count, seqs, chunk, key_cols)

    key_terms = jnp.concatenate([key_blocks(grad_k), key_blocks(grad_v)], axis=3)
    key_owned = line_sum(line_send(key_terms))
    key_owned, own_gate = tie(key_owned, own_gate)
    grad_q_pre = rope_back(
        join_heads(grad_q).reshape(seqs, chunk, query_heads, HEAD), cosine, sine
    )
    grad_k_pre = rope_back(
        key_owned[:, :, :key_cols].reshape(seqs, chunk, own_keys, HEAD), cosine, sine
    )
    grad_projected = jnp.concatenate(
        [
            grad_q_pre.reshape(rows, query_cols),
            grad_k_pre.reshape(rows, key_cols),
            key_owned[:, :, key_cols:].reshape(rows, key_cols),
        ],
        axis=1,
    ).astype(jnp.bfloat16)
    grad_attn_in = outer_sum(normed_one_all, grad_projected)
    grad_normed_one = plane_scatter(grad_projected, attn_in, True)
    grad_normed_one, own_up, *output_tiles = tie(grad_normed_one, own_up, *output_tiles)
    output = place_tiles(output_tiles)
    grad_stream_one, grad_norm1 = norm_backward(stream, inverse_one, gain_one, grad_normed_one)
    input_grad = place_tiles(send_tiles((grad_one + grad_stream_one).astype(jnp.bfloat16)))

    def spread_keys(own):
        if share == 1:
            return spread(own, 1)
        every = lax.all_gather(own, "dp", axis=0).astype(jnp.float32)
        every = every.reshape(dp_count // share, share, -1, key_cols).sum(axis=1)
        return every.transpose(1, 0, 2).reshape(every.shape[1], -1)

    def own_norm(total):
        return plane_sum(line_sum(line_send(total.reshape(mx_count, -1))))

    grad_down = spread(own_down, 0)
    grad_gate = spread(own_gate, 1)
    grad_up = spread(own_up, 1)
    grad_out = spread(line_scatter(grad_out, 1), 0)
    own_attn = line_scatter(grad_attn_in, 0)
    grad_query = spread(own_attn[:, :query_cols], 1)
    grad_key = spread_keys(own_attn[:, query_cols : query_cols + key_cols])
    grad_value = spread_keys(own_attn[:, query_cols + key_cols :])
    grad_norm2 = own_norm(grad_norm2)
    grad_norm1 = own_norm(grad_norm1)
    return (
        output,
        input_grad,
        grad_norm1,
        grad_query,
        grad_key,
        grad_value,
        grad_out,
        grad_norm2,
        grad_gate,
        grad_up,
        grad_down,
    )


def solution(mesh):
    placed = (
        P(("dp", "my"), "mx"),
        P(("dp", "my"), "mx"),
        P("dp", None),
        P("mx"),
        P("mx", "my"),
        P("mx", "my"),
        P("mx", "my"),
        P("my", "mx"),
        P("mx"),
        P("mx", "my"),
        P("mx", "my"),
        P("my", "mx"),
    )
    return jax.shard_map(
        shards,
        mesh=mesh,
        in_specs=placed,
        out_specs=(
            P(("dp", "my"), "mx"),
            P(("dp", "my"), "mx"),
            P("mx"),
            P("mx", "my"),
            P("mx", "my"),
            P("mx", "my"),
            P("my", "mx"),
            P("mx"),
            P("mx", "my"),
            P("mx", "my"),
            P("my", "mx"),
        ),
        check_vma=False,
    )
```

```python
import functools

import jax
import jax.numpy as jnp
from jax import lax
from jax.experimental import pallas as pl
from jax.experimental.pallas import tpu as pltpu
from jax.sharding import PartitionSpec as P

D = 2048
HEAD = 64
LEN = 1024
PIECE = 256


epsilon = 1e-05
rope_base = 10000000.0
branch_scale = 0.22
score_scale = 0.015625
masked_score = -1e30


def rope_tables(positions, head_width):
    half_width = head_width // 2
    steps_idx = jnp.arange(half_width, dtype=jnp.float32)
    freqs = jnp.exp(-jnp.log(jnp.float32(rope_base)) * 2.0 * steps_idx / head_width)
    angles = positions.astype(jnp.float32)[:, None] * freqs[None, :]
    cosine = jnp.cos(angles)
    sine = jnp.sin(angles)
    return (jnp.concatenate([cosine, cosine], 1), jnp.concatenate([sine, sine], 1))


def rotate_half(values):
    half_width = values.shape[-1] // 2
    return jnp.concatenate([-values[..., half_width:], values[..., :half_width]], -1)


def apply_rope(values, cosine, sine):
    return values * cosine + rotate_half(values) * sine


def rope_back(values, cosine, sine):
    return values * cosine - rotate_half(values) * sine


def product(left, weight, flipped):
    if flipped:
        return lax.dot_general(
            left, weight, (((1,), (1,)), ((), ())), preferred_element_type=jnp.float32
        )
    return jnp.dot(left, weight, preferred_element_type=jnp.float32)


def outer_sum(left, right):
    return lax.dot_general(
        left, right, (((0,), (0,)), ((), ())), preferred_element_type=jnp.float32
    )


def score_bias(starts_ref, offset_ref, seq, chunk, pieces):
    query_pos = offset_ref[0] + lax.broadcasted_iota(jnp.int32, (1, chunk), 1)
    key_pos = lax.broadcasted_iota(jnp.int32, (LEN, 1), 0)
    query_piece = jnp.zeros((1, chunk), jnp.int32)
    key_piece = jnp.full((LEN, 1), -1, jnp.int32)
    for p in range(pieces):
        begin = starts_ref[seq * pieces + p]
        inside = (query_pos >= begin) & (query_pos < begin + PIECE)
        query_piece = jnp.where(inside, p + 1, query_piece)
        inside = (key_pos >= begin) & (key_pos < begin + PIECE)
        key_piece = jnp.where(inside, p + 1, key_piece)
    seen = (key_pos <= query_pos) | (key_piece == query_piece)
    return jnp.where(seen, 0.0, masked_score).astype(jnp.float32)


def dot_rows(left, right):
    return jnp.dot(left, right, preferred_element_type=jnp.float32)


def attend_kernel(starts_ref, offset_ref, query_ref, key_ref, value_ref, out_ref, total_ref, *, own_keys, group, pieces):
    chunk = query_ref.shape[2] // group
    bias = score_bias(starts_ref, offset_ref, pl.program_id(0) // own_keys, chunk, pieces)
    key = key_ref[0]
    value = value_ref[0]
    for g in range(group):
        at = slice(g * chunk, (g + 1) * chunk)
        scores = dot_rows(key, query_ref[0, :, at]) * score_scale + bias
        top = jnp.max(scores, axis=0, keepdims=True)
        shifted = jnp.exp(scores - top)
        total = jnp.sum(shifted, axis=0, keepdims=True)
        probs = (shifted * (1.0 / total)).astype(jnp.bfloat16)
        out_ref[0, :, at] = dot_rows(value, probs).astype(jnp.bfloat16)
        total_ref[0, :, at] = top + jnp.log(total)


def attend_back_kernel(
    starts_ref, offset_ref, query_ref, rows_ref, key_ref, value_ref, keyt_ref, grad_ref,
    grad_rows_ref, total_ref, dq_ref, dk_ref, dv_ref, *, own_keys, group, pieces
):
    chunk = query_ref.shape[2] // group
    bias = score_bias(starts_ref, offset_ref, pl.program_id(0) // own_keys, chunk, pieces)
    key = key_ref[0]
    value = value_ref[0]
    keyt = keyt_ref[0]
    grad_key = jnp.zeros(key.shape, jnp.float32)
    grad_value = jnp.zeros(key.shape, jnp.float32)
    for g in range(group):
        at = slice(g * chunk, (g + 1) * chunk)
        scores = dot_rows(key, query_ref[0, :, at]) * score_scale + bias
        probs = jnp.exp(scores - total_ref[0, :, at])
        grad_probs = dot_rows(value, grad_ref[0, :, at])
        scaled = probs * grad_probs
        row_dot = jnp.sum(scaled, axis=0, keepdims=True)
        grad_scores = (scaled - probs * row_dot).astype(jnp.bfloat16)
        dq_ref[0, :, at] = dot_rows(keyt, grad_scores) * score_scale
        grad_key = grad_key + dot_rows(grad_scores, rows_ref[0, at, :])
        grad_value = grad_value + dot_rows(probs.astype(jnp.bfloat16), grad_rows_ref[0, at, :])
    dk_ref[0] = (grad_key * score_scale).astype(jnp.bfloat16)
    dv_ref[0] = grad_value.astype(jnp.bfloat16)


def whole_block(array):
    return pl.BlockSpec((1,) + array.shape[1:], lambda i: (i, 0, 0))


def attend_call(kernel, starts, offset, arrays, outs, own_keys, group, flops):
    smem = pl.BlockSpec(memory_space=pltpu.SMEM)
    return pl.pallas_call(
        functools.partial(kernel, own_keys=own_keys, group=group, pieces=starts.shape[-1]),
        grid=(arrays[0].shape[0],),
        in_specs=[smem, smem] + [whole_block(a) for a in arrays],
        out_specs=[whole_block(o) for o in outs],
        out_shape=outs,
        cost_estimate=pl.CostEstimate(flops=flops, transcendentals=0, bytes_accessed=0),
    )(starts.reshape(-1), offset.reshape(1), *arrays)


PLANE = ("dp", "my")


def swap(values, bit):
    count = lax.axis_size("dp")
    return lax.ppermute(values, "dp", [(i, i ^ bit) for i in range(count)])


def swap_core(values):
    count = lax.axis_size("my")
    return lax.ppermute(values, "my", [(i, i ^ 1) for i in range(count)])


def small_plane():
    return lax.axis_size("dp") == 4 and lax.axis_size("my") == 2


def plane_gather(values):
    if not small_plane():
        return lax.all_gather(values, PLANE, axis=0, tiled=True)
    half = values.shape[0] // 2
    from_x = swap(values, 1)
    from_y = swap(values, 2)
    core_own = swap_core(values)
    corner_low = swap(from_y[:half], 1)
    corner_high = swap(from_x[half:], 2)
    core_x = swap_core(from_x)
    core_y = swap_core(from_y)
    corner = jnp.concatenate([corner_low, corner_high], axis=0)
    core_corner = swap_core(corner)
    return jnp.concatenate(
        [values, from_x, from_y, corner, core_own, core_x, core_y, core_corner], axis=0
    )


def plane_products(left, weight, flipped):
    if not small_plane():
        return (product(left, weight, flipped).astype(jnp.bfloat16),)
    middle = left.shape[0] // 2
    other = product(left[middle:], weight, flipped).astype(jnp.bfloat16)
    return (other, product(left[:middle], weight, flipped).astype(jnp.bfloat16))


def plane_scatter(left, weight, flipped):
    return plane_reduce(*plane_products(left, weight, flipped))


def plane_reduce(*products):
    if not small_plane():
        return lax.psum_scatter(
            products[0],
            PLANE,
            scatter_dimension=0,
            tiled=True,
        ).astype(jnp.float32)
    other, own = products
    rows = own.shape[0] // 4
    half = rows // 2
    low = jnp.bfloat16
    wide = jnp.float32
    got = [swap_core(other[k * rows : (k + 1) * rows]) for k in range(4)]
    part = [
        own[k * rows : (k + 1) * rows].astype(wide) + got[k].astype(wide) for k in range(4)
    ]
    via_x = swap(jnp.concatenate([part[3][:half], part[1][:half]], 0).astype(low), 1).astype(wide)
    via_y = swap(jnp.concatenate([part[3][half:], part[2][half:]], 0).astype(low), 2).astype(wide)
    next_y = swap((part[2][:half] + via_x[:half]).astype(low), 2)
    next_x = swap((part[1][half:] + via_y[:half]).astype(low), 1)
    first = part[0][:half] + via_x[half:] + next_y.astype(wide)
    second = part[0][half:] + via_y[half:] + next_x.astype(wide)
    return jnp.concatenate([first, second], axis=0)


def plane_starts(starts):
    if not small_plane():
        return lax.all_gather(starts, "dp", axis=0, tiled=True)
    from_x = swap(starts, 1)
    from_y = swap(starts, 2)
    every = jnp.stack([starts, from_x, from_y, swap(from_y, 1)])
    my_index = lax.axis_index("my")
    return jnp.concatenate([every[:, my_index], every[:, my_index ^ 1]], axis=0)


def plane_sum(values):
    if not small_plane():
        return lax.psum(values, PLANE)
    values = values + swap_core(values)
    values = values + swap(values, 1)
    return values + swap(values, 2)


def dp_first(own):
    if not small_plane():
        return (own,)
    return (own, swap(own, 1), swap(own, 2))


def dp_blocks(own, from_x=None, from_y=None):
    index = lax.axis_index("dp")
    if from_x is None:
        every = lax.all_gather(own, "dp", axis=0)
        return [(k, every[k]) for k in range(every.shape[0])]
    half = own.shape[0] // 2
    corner_low = swap(from_y[:half], 1)
    corner_high = swap(from_x[half:], 2)
    corner = jnp.concatenate([corner_low, corner_high], axis=0)
    return [(index ^ k, b) for k, b in enumerate([own, from_x, from_y, corner])]


def spread(first, axis):
    own = first[0]
    shape = list(own.shape)
    shape[axis] *= lax.axis_size("dp")
    result = jnp.zeros(shape, jnp.float32)
    for index, block in dp_blocks(*first):
        result = lax.dynamic_update_slice_in_dim(
            result, block.astype(jnp.float32), index * own.shape[axis], axis
        )
    return result


def tie(value, *after):
    return lax.optimization_barrier((value,) + after)


def line_send(blocks):
    count = lax.axis_size("mx")
    index = lax.axis_index("mx")

    def at(offset):
        return lax.dynamic_index_in_dim(blocks, (index + offset) % count, 0, keepdims=False)

    return [at(0)] + [
        lax.ppermute(at(shift), "mx", [(i, (i + shift) % count) for i in range(count)])
        for shift in range(1, count)
    ]


def line_place(received):
    count = len(received)
    index = lax.axis_index("mx")
    placed = []
    for place in range(count):
        turn = (index - place) % count
        block = received[0]
        for r in range(1, count):
            block = jnp.where(turn == r, received[r], block)
        placed.append(block)
    return placed


def line_sum(received):
    total = received[0].astype(jnp.float32)
    for block in received[1:]:
        total = total + block.astype(jnp.float32)
    return total


def send_rows(values):
    return line_send(values.reshape(lax.axis_size("mx"), -1, values.shape[1]))


def place_rows(received):
    return jnp.concatenate(line_place(received), axis=1)


def send_tiles(values):
    count = lax.axis_size("mx")
    return line_send(values.reshape(values.shape[0], count, -1).transpose(1, 0, 2))


def place_tiles(received):
    return jnp.concatenate(line_place(received), axis=0)


def line_gather(values, axis):
    return lax.all_gather(values, "mx", axis=axis, tiled=True)


def line_scatter(values, axis):
    return lax.psum_scatter(
        values.astype(jnp.bfloat16), "mx", scatter_dimension=axis, tiled=True
    )


def norm_forward(stream, gain):
    mean = jnp.mean(stream * stream, axis=1, keepdims=True)
    inverse = lax.rsqrt(mean + epsilon)
    return (inverse, (stream * inverse * gain[None, :]).astype(jnp.bfloat16))


def norm_backward(stream, inverse, gain, grad_normed):
    scaled = gain[None, :] * grad_normed
    row_mean = jnp.mean(stream * scaled, axis=1, keepdims=True)
    grad_stream = inverse * scaled - stream * inverse * inverse * inverse * row_mean
    grad_gain = jnp.sum(grad_normed * stream * inverse, axis=0)
    return (grad_stream, grad_gain)


def shards(
    tokens,
    output_grad,
    picture_starts,
    norm1_gain,
    query_weight,
    key_weight,
    value_weight,
    out_weight,
    norm2_gain,
    gate_weight,
    up_weight,
    down_weight,
):
    mx_count = lax.axis_size("mx")
    dp_count = lax.axis_size("dp")
    dp_index = lax.axis_index("dp")
    mx_index = lax.axis_index("mx")
    chunk = LEN // mx_count
    seqs = dp_count * lax.axis_size("my")
    rows = seqs * chunk
    query_cols = query_weight.shape[1] // dp_count
    query_heads = query_cols // HEAD
    key_heads = key_weight.shape[1] // HEAD
    share = max(1, dp_count // key_heads)
    key_cols = key_weight.shape[1] * share // dp_count
    own_keys = key_cols // HEAD
    kv_group = query_heads // own_keys
    hidden = gate_weight.shape[1] // dp_count

    def cols(weight, width, index):
        return lax.dynamic_slice_in_dim(weight, index * width, width, axis=1)

    def rows_of(weight, width):
        return lax.dynamic_slice_in_dim(weight, dp_index * width, width, axis=0)

    key_index = dp_index // share
    attn_cols = query_cols + 2 * key_cols
    attn_all = line_gather(
        jnp.concatenate(
            [
                cols(query_weight, query_cols, dp_index),
                cols(key_weight, key_cols, key_index),
                cols(value_weight, key_cols, key_index),
                rows_of(out_weight, query_cols).T,
            ],
            axis=1,
        ),
        0,
    )
    attn_in = attn_all[:, :attn_cols]
    attn_back = attn_all[:, attn_cols:]
    gains = jnp.stack([norm1_gain, norm2_gain])
    gains = line_place(line_send(jnp.broadcast_to(gains, (mx_count,) + gains.shape)))
    gain_one, gain_two = jnp.concatenate(gains, axis=1)
    starts = plane_starts(picture_starts)

    stream = place_rows(send_rows(tokens)).astype(jnp.float32)
    inverse_one, normed_one = norm_forward(stream, gain_one)
    normed_one_all = plane_gather(normed_one)
    projected = product(normed_one_all, attn_in, False)

    query_pos = mx_index * chunk + jnp.arange(chunk, dtype=jnp.int32)
    cosine, sine = rope_tables(query_pos, HEAD)
    cosine = cosine[None, :, None, :]
    sine = sine[None, :, None, :]
    query_rot = apply_rope(
        projected[:, :query_cols].reshape(seqs, chunk, query_heads, HEAD), cosine, sine
    ).astype(jnp.bfloat16)
    key_rot = apply_rope(
        projected[:, query_cols : query_cols + key_cols].reshape(seqs, chunk, own_keys, HEAD),
        cosine,
        sine,
    ).astype(jnp.bfloat16)
    value_own = projected[:, query_cols + key_cols :].astype(jnp.bfloat16)
    key_local = jnp.concatenate(
        [key_rot.reshape(seqs, chunk, key_cols), value_own.reshape(seqs, chunk, key_cols)], axis=2
    )
    key_all = line_gather(key_local, 1)
    down_rows, stream = tie(rows_of(down_weight, hidden), stream)
    ffn_back = line_gather(down_rows, 1)
    ffn_cols = jnp.concatenate(
        [cols(gate_weight, hidden, dp_index), cols(up_weight, hidden, dp_index)], axis=1
    )
    key_all, ffn_cols, late_grad = tie(key_all, ffn_cols, output_grad)
    ffn_in = line_gather(ffn_cols, 0)
    grad_rows = send_rows(late_grad)

    def head_cols(values):
        values = values.reshape(seqs, chunk, own_keys, kv_group, HEAD).transpose(0, 2, 4, 3, 1)
        return values.reshape(-1, HEAD, kv_group * chunk)

    def head_rows(values):
        values = values.reshape(seqs, chunk, own_keys, kv_group, HEAD).transpose(0, 2, 3, 1, 4)
        return values.reshape(-1, kv_group * chunk, HEAD)

    def join_heads(values):
        values = values.reshape(seqs, own_keys, HEAD, kv_group, chunk).transpose(0, 4, 1, 3, 2)
        return values.reshape(rows, query_cols)

    def split_keys(values):
        values = values.reshape(seqs, LEN, own_keys, HEAD)
        return values.transpose(0, 2, 1, 3).reshape(-1, LEN, HEAD)

    query_split = head_cols(query_rot)
    key_split = split_keys(key_all[:, :, :key_cols])
    value_split = split_keys(key_all[:, :, key_cols:])
    offset = mx_index * chunk
    work = 2 * seqs * chunk * query_cols * LEN
    mixed, log_totals = attend_call(
        attend_kernel,
        starts,
        offset,
        [query_split, key_split, value_split.transpose(0, 2, 1)],
        [
            jax.ShapeDtypeStruct(query_split.shape, jnp.bfloat16),
            jax.ShapeDtypeStruct((query_split.shape[0], 1, query_split.shape[2]), jnp.float32),
        ],
        own_keys,
        kv_group,
        2 * work,
    )
    attn_out = join_heads(mixed)
    hidden_one = stream + branch_scale * plane_scatter(attn_out, attn_back, True)
    inverse_two, normed_two = norm_forward(hidden_one, gain_two)
    normed_two_all, *grad_rows = tie(plane_gather(normed_two), *grad_rows)
    grad_two = place_rows(grad_rows).astype(jnp.float32)
    gate_up = product(normed_two_all, ffn_in, False)
    gate_val = gate_up[:, :hidden]
    up_val = gate_up[:, hidden:]
    sigma = jax.nn.sigmoid(gate_val)
    silu_gate = gate_val * sigma
    hidden_units = (silu_gate * up_val).astype(jnp.bfloat16)
    down_products = plane_products(hidden_units, ffn_back, False)

    branch_two = (branch_scale * grad_two).astype(jnp.bfloat16)
    branch_two_all = plane_gather(branch_two)
    grad_down = outer_sum(hidden_units, branch_two_all)
    grad_hidden = product(branch_two_all, ffn_back, True)
    grad_gate_val = (grad_hidden * up_val * sigma * (1.0 + gate_val * (1.0 - sigma))).astype(
        jnp.bfloat16
    )
    grad_up_val = (grad_hidden * silu_gate).astype(jnp.bfloat16)
    grad_gate_up = jnp.concatenate([grad_gate_val, grad_up_val], axis=1)
    grad_normed_two = plane_scatter(grad_gate_up, ffn_in, True)
    own_down = line_scatter(grad_down, 1)
    own_gate = line_scatter(outer_sum(normed_two_all, grad_gate_val), 0)
    own_up = line_scatter(outer_sum(normed_two_all, grad_up_val), 0)
    grad_stream_two, grad_norm2 = norm_backward(hidden_one, inverse_two, gain_two, grad_normed_two)
    grad_one = grad_two + grad_stream_two
    branch_one_all = plane_gather((branch_scale * grad_one).astype(jnp.bfloat16))
    branch_one_all, *down_products = tie(branch_one_all, *down_products)
    hidden_two = hidden_one + branch_scale * plane_reduce(*down_products)
    output_tiles = send_tiles(hidden_two.astype(jnp.bfloat16))
    grad_attn = product(branch_one_all, attn_back, False).astype(jnp.bfloat16)
    grad_cols, grad_heads = head_cols(grad_attn), head_rows(grad_attn)
    like_key = jax.ShapeDtypeStruct(key_split.shape, jnp.bfloat16)
    grad_q, grad_k, grad_v = attend_call(
        attend_back_kernel,
        starts,
        offset,
        [
            query_split,
            head_rows(query_rot),
            key_split,
            value_split,
            key_split.transpose(0, 2, 1),
            grad_cols,
            grad_heads,
            log_totals,
        ],
        [jax.ShapeDtypeStruct(query_split.shape, jnp.float32), like_key, like_key],
        own_keys,
        kv_group,
        5 * work,
    )
    grad_k, own_down, own_gate, own_up = tie(grad_k, own_down, own_gate, own_up)
    down_first = dp_first(own_down)

    def key_blocks(values):
        values = values.reshape(seqs, own_keys, mx_count, chunk, HEAD).transpose(2, 0, 3, 1, 4)
        return values.reshape(mx_count, seqs, chunk, key_cols)

    key_terms = jnp.concatenate([key_blocks(grad_k), key_blocks(grad_v)], axis=3)
    key_owned = lax.psum_scatter(key_terms, "mx", scatter_dimension=0).astype(jnp.float32)
    key_owned, attn_late, own_gate, own_up, *down_first = tie(
        key_owned, attn_out, own_gate, own_up, *down_first
    )
    gate_first = dp_first(own_gate)
    up_first = dp_first(own_up)
    grad_out = outer_sum(attn_late, branch_one_all)
    grad_q_pre = rope_back(
        join_heads(grad_q).reshape(seqs, chunk, query_heads, HEAD), cosine, sine
    )
    grad_k_pre = rope_back(
        key_owned[:, :, :key_cols].reshape(seqs, chunk, own_keys, HEAD), cosine, sine
    )
    grad_projected = jnp.concatenate(
        [
            grad_q_pre.reshape(rows, query_cols),
            grad_k_pre.reshape(rows, key_cols),
            key_owned[:, :, key_cols:].reshape(rows, key_cols),
        ],
        axis=1,
    ).astype(jnp.bfloat16)
    grad_attn_in = outer_sum(normed_one_all, grad_projected)
    grad_normed_one = plane_scatter(grad_projected, attn_in, True)
    grad_normed_one, *output_tiles = tie(grad_normed_one, *output_tiles)
    output = place_tiles(output_tiles)
    grad_stream_one, grad_norm1 = norm_backward(stream, inverse_one, gain_one, grad_normed_one)
    input_grad = place_tiles(send_tiles((grad_one + grad_stream_one).astype(jnp.bfloat16)))

    def spread_keys(own):
        if share == 1:
            return spread(dp_first(own), 1)
        every = lax.all_gather(own, "dp", axis=0).astype(jnp.float32)
        every = every.reshape(dp_count // share, share, -1, key_cols).sum(axis=1)
        return every.transpose(1, 0, 2).reshape(every.shape[1], -1)

    def own_norm(total):
        return plane_sum(line_sum(line_send(total.reshape(mx_count, -1))))

    grad_down = spread(down_first, 0)
    grad_gate = spread(gate_first, 1)
    grad_up = spread(up_first, 1)
    grad_out = spread(dp_first(line_scatter(grad_out, 1)), 0)
    own_attn = line_scatter(grad_attn_in, 0)
    grad_query = spread(dp_first(own_attn[:, :query_cols]), 1)
    grad_key = spread_keys(own_attn[:, query_cols : query_cols + key_cols])
    grad_value = spread_keys(own_attn[:, query_cols + key_cols :])
    grad_norm2 = own_norm(grad_norm2)
    grad_norm1 = own_norm(grad_norm1)
    return (
        output,
        input_grad,
        grad_norm1,
        grad_query,
        grad_key,
        grad_value,
        grad_out,
        grad_norm2,
        grad_gate,
        grad_up,
        grad_down,
    )


def solution(mesh):
    placed = (
        P(("dp", "my"), "mx"),
        P(("dp", "my"), "mx"),
        P("dp", None),
        P("mx"),
        P("mx", "my"),
        P("mx", "my"),
        P("mx", "my"),
        P("my", "mx"),
        P("mx"),
        P("mx", "my"),
        P("mx", "my"),
        P("my", "mx"),
    )
    return jax.shard_map(
        shards,
        mesh=mesh,
        in_specs=placed,
        out_specs=(
            P(("dp", "my"), "mx"),
            P(("dp", "my"), "mx"),
            P("mx"),
            P("mx", "my"),
            P("mx", "my"),
            P("mx", "my"),
            P("my", "mx"),
            P("mx"),
            P("mx", "my"),
            P("mx", "my"),
            P("my", "mx"),
        ),
        check_vma=False,
    )
```
